128 devices in a mesh: section: 4 (over z_lo, core), expert: 32 (over y, x, z_hi).
Axes of the slice: x: 4, y: 4, z: 4 (z_hi: 2, z_lo: 2; z = z_hi * 2 + z_lo), core: 2. Of those that a mesh axis runs over, the one named last changes fastest.
Arguments:
- tokens: bfloat16 [4, 2048, 4096], P('section', 'expert'), may hold values from -6 to 6
- out_grad: bfloat16 [4, 2048, 4096], P('section', 'expert'), may hold values from -6 to 6
- expert_ids: int32 [4, 2048, 2], P('section', 'expert'), may hold values from 0 to 7, as said below
- slot_ids: int32 [4, 2048, 2], P('section', 'expert'), may hold values from 0 to 15, as said below
- gate_int: int32 [4, 2048, 2], P('section', 'expert'), may hold values from 16 to 255
- saved_gate: bfloat16 [4, 512, 14336], P('section', None, 'expert'), may hold values from -6 to 6
- saved_up: bfloat16 [4, 512, 14336], P('section', None, 'expert'), may hold values from -6 to 6
- w_gate: bfloat16 [4, 4096, 14336], P('section', None, 'expert'), may hold values from -0.09375 to 0.09375
- w_up: bfloat16 [4, 4096, 14336], P('section', None, 'expert'), may hold values from -0.09375 to 0.09375
- w_down: bfloat16 [4, 14336, 4096], P('section', 'expert'), may hold values from -0.0625 to 0.0625
Outputs:
- arriving_grad: bfloat16 [4, 2048, 4096], P('section', 'expert')
- grad_w_gate: bfloat16 [4, 4096, 14336], P('section', None, 'expert')
- grad_w_up: bfloat16 [4, 4096, 14336], P('section', None, 'expert')
- grad_w_down: bfloat16 [4, 14336, 4096], P('section', 'expert')
The draws below stay inside these ranges and needn't reach their ends.
Inputs may be any that keep to these rules, and one draw needn't show every extreme that they name: `expert_ids`: in each section, the 64 tokens of each index of expert name each of the 8 experts exactly 16 times; a token's two experts differ. `slot_ids`: for each expert, the slots of the 64 tokens of one index of expert that name it are 0 to 15, each once.
All inputs are finite; a program needn't handle non-finite values.
Results may differ from the reference program's by a relative error of at most 0.018.
Values may be sent and summed in bfloat16 or wider, within the bound.
A program may use at most 128 MiB of HBM per device.

```python
import jax
import jax.numpy as jnp
from jax import lax

D = 4096
EXPERTS = 8
H_WIN = 7168
E_WIN = 2
TOK_DEV = 64
CAP = 16
TOKENS = 2048
SECTIONS = 4
N_EXPERT = 32


def routing_tables(key):
    blocks = SECTIONS * (TOKENS // TOK_DEV)

    def one_block(block_key):
        rank_key, label_key, slot_key = jax.random.split(block_key, 3)
        token_rank = jax.random.permutation(rank_key, TOK_DEV).astype(jnp.int32)
        relabel = jax.random.permutation(label_key, EXPERTS).astype(jnp.int32)
        slot_perms = jax.vmap(lambda one_key: jax.random.permutation(one_key, CAP).astype(jnp.int32))(jax.random.split(slot_key, EXPERTS))
        lane_index = token_rank % EXPERTS
        rounds = token_rank // EXPERTS
        second = (lane_index + 1 + rounds % (EXPERTS - 1)) % EXPERTS
        chosen = jnp.stack([relabel[lane_index], relabel[second]], axis=-1)
        first_slot = slot_perms[lane_index, rounds]
        second_slot = slot_perms[second, TOK_DEV // EXPERTS + rounds]
        places = jnp.stack([first_slot, second_slot], axis=-1)
        return (chosen, places)
    chosen, places = jax.vmap(one_block)(jax.random.split(key, blocks))
    return (chosen.reshape(SECTIONS, TOKENS, 2).astype(jnp.int32), places.reshape(SECTIONS, TOKENS, 2).astype(jnp.int32))


def draw_expert_ids(key, part):
    return routing_tables(jax.random.fold_in(key, 17))[0]


def draw_slot_ids(key, part):
    return routing_tables(jax.random.fold_in(key, 17))[1]


def plant(array, key, smallest, largest):
    shape = array.shape
    index_at = [jax.random.randint(jax.random.fold_in(key, axis), (), 0, shape[axis]) for axis in range(len(shape))]
    array = array.at[tuple(index_at)].set(smallest)
    longest = shape.index(max(shape))
    index_at[longest] = (index_at[longest] + 1) % shape[longest]
    return array.at[tuple(index_at)].set(largest)


def levels(key, extent, pieces, smallest, largest):
    def one(dim, shards_of):
        steps = jax.random.uniform(jax.random.fold_in(jax.random.fold_in(key, 6), dim), (shards_of,), jnp.float32, smallest / len(pieces), largest / len(pieces))
        return jnp.repeat(jnp.exp(steps), extent[dim] // shards_of).reshape((-1,) + (1,) * (len(extent) - dim - 1))

    gain = one(*pieces[0])
    for cut in pieces[1:]:
        gain = gain * one(*cut)
    return gain


def bell_draw(key, dims, width, reach, pieces=(), held_as=jnp.bfloat16):
    values = width * jax.random.normal(key, dims, jnp.float32)
    if pieces:
        values = values * levels(key, dims, pieces, -0.22, 0.18)
    return jnp.clip(values, -reach, reach).astype(held_as)


def setup_inputs(seed: int = 0) -> dict:
    streams_of = jax.random.split(jax.random.key(seed), 11)
    tokens = bell_draw(streams_of[0], (SECTIONS, TOKENS, D), 1.0, 6.0, ((0, 4), (1, 32)))
    out_grad = bell_draw(streams_of[1], (SECTIONS, TOKENS, D), 1.0, 6.0, ((0, 4), (1, 32)))
    expert_ids = draw_expert_ids(jax.random.fold_in(streams_of[10], 71), 0)
    slot_ids = draw_slot_ids(jax.random.fold_in(streams_of[10], 71), 0)
    gate_int = plant(jax.random.randint(streams_of[4], (SECTIONS, TOKENS, 2), 16, 256), jax.random.fold_in(streams_of[4], 1), 16, 255).astype(jnp.int32)
    saved_gate = bell_draw(streams_of[5], (SECTIONS, N_EXPERT * CAP, E_WIN * H_WIN), 1.5, 6.0, ((0, 4), (2, 32)))
    saved_up = bell_draw(streams_of[6], (SECTIONS, N_EXPERT * CAP, E_WIN * H_WIN), 1.0, 6.0, ((0, 4), (2, 32)))
    w_gate = bell_draw(streams_of[7], (SECTIONS, D, E_WIN * H_WIN), D ** -0.5, 0.09375, ((0, 4), (2, 32)))
    w_up = bell_draw(streams_of[8], (SECTIONS, D, E_WIN * H_WIN), D ** -0.5, 0.09375, ((0, 4), (2, 32)))
    w_down = bell_draw(streams_of[9], (SECTIONS, E_WIN * H_WIN, D), H_WIN ** -0.5, 0.0625, ((0, 4), (1, 32)))
    return {"tokens": tokens, "out_grad": out_grad, "expert_ids": expert_ids, "slot_ids": slot_ids, "gate_int": gate_int, "saved_gate": saved_gate, "saved_up": saved_up, "w_gate": w_gate, "w_up": w_up, "w_down": w_down}


def section_grads(inputs, upstream_grad, chosen, places, gate_int, saved_gate, saved_up, w_gate, w_up, w_down):
    per_expert = N_EXPERT // E_WIN
    shard_width = H_WIN // per_expert
    row_total = N_EXPERT * CAP
    block_of = (jnp.arange(TOKENS, dtype=jnp.int32) // TOK_DEV)[:, None]
    weights_k = gate_int.astype(jnp.float32) / 256.0
    gated = (upstream_grad.astype(jnp.float32)[:, None, :] * weights_k[:, :, None]).astype(jnp.bfloat16)
    repeated = jnp.broadcast_to(inputs[:, None, :], (TOKENS, 2, D))
    result = jnp.zeros((TOKENS, D), jnp.float32)
    grads_gate = []
    grads_up = []
    grads_down = []
    for expert_num in range(E_WIN):
        hit = chosen == expert_num
        target = jnp.where(hit, block_of * CAP + places, row_total).astype(jnp.int32)
        flat_rows = target.reshape(-1)
        rows_in = jnp.zeros((row_total, D), jnp.bfloat16).at[flat_rows].set(repeated.reshape(-1, D), mode="drop")
        rows_grad = jnp.zeros((row_total, D), jnp.bfloat16).at[flat_rows].set(gated.reshape(-1, D), mode="drop")
        first = expert_num * H_WIN
        gate_pre = saved_gate[:, first:first + H_WIN].astype(jnp.float32)
        up_pre = saved_up[:, first:first + H_WIN].astype(jnp.float32)
        sigmoid_g = jax.nn.sigmoid(gate_pre)
        activated = gate_pre * sigmoid_g
        hidden = (activated * up_pre).astype(jnp.bfloat16)
        hidden_grad = jnp.dot(rows_grad, w_down[first:first + H_WIN, :].T, preferred_element_type=jnp.float32)
        gate_grad = (hidden_grad * up_pre * sigmoid_g * (1.0 + gate_pre * (1.0 - sigmoid_g))).astype(jnp.bfloat16)
        up_grad = (hidden_grad * activated).astype(jnp.bfloat16)
        grads_down.append(jnp.dot(hidden.T, rows_grad, preferred_element_type=jnp.float32).astype(jnp.bfloat16))
        grads_gate.append(jnp.dot(rows_in.T, gate_grad, preferred_element_type=jnp.float32).astype(jnp.bfloat16))
        grads_up.append(jnp.dot(rows_in.T, up_grad, preferred_element_type=jnp.float32).astype(jnp.bfloat16))
        gate_parts = jnp.einsum("rgh,dgh->grd", gate_grad.astype(jnp.float32).reshape(row_total, per_expert, shard_width), w_gate[:, first:first + H_WIN].astype(jnp.float32).reshape(D, per_expert, shard_width))
        parts = gate_parts + jnp.einsum("rgh,dgh->grd", up_grad.astype(jnp.float32).reshape(row_total, per_expert, shard_width), w_up[:, first:first + H_WIN].astype(jnp.float32).reshape(D, per_expert, shard_width))
        rounded = lax.optimization_barrier(parts.astype(jnp.bfloat16))
        summed = jnp.sum(rounded.astype(jnp.float32), axis=0)
        picked = summed[jnp.minimum(target, row_total - 1)]
        result = result + jnp.sum(jnp.where(hit[:, :, None], picked, jnp.float32(0.0)), axis=1)
    input_grad = result.astype(jnp.bfloat16)
    return input_grad, jnp.concatenate(grads_gate, axis=1), jnp.concatenate(grads_up, axis=1), jnp.concatenate(grads_down, axis=0)


def reference(tokens, out_grad, expert_ids, slot_ids, gate_int, saved_gate, saved_up, w_gate, w_up, w_down):
    input_grads = []
    all_gate = []
    all_up = []
    all_down = []
    for layer_index in range(SECTIONS):
        outcome = section_grads(tokens[layer_index], out_grad[layer_index], expert_ids[layer_index], slot_ids[layer_index], gate_int[layer_index], saved_gate[layer_index], saved_up[layer_index], w_gate[layer_index], w_up[layer_index], w_down[layer_index])
        input_grads.append(outcome[0])
        all_gate.append(outcome[1])
        all_up.append(outcome[2])
        all_down.append(outcome[3])
    arriving = input_grads[1:] + [jnp.zeros((TOKENS, D), jnp.bfloat16)]
    return jnp.stack(arriving), jnp.stack(all_gate), jnp.stack(all_up), jnp.stack(all_down)
```

```python
import jax
import jax.numpy as jnp
from jax import lax
from jax.experimental import pallas as pl
from jax.experimental.pallas import tpu as pltpu
from jax.sharding import PartitionSpec as P

E_WIN = 2
CAP = 16
ROWS = 512
Y_OF_CHUNK = (0, 3, 1, 2)
COPIES = 80


def kernel(
    ids_ref, slots_ref, gates_ref, tok_hbm, og_hbm, sg_hbm, su_hbm, wg_hbm, wu_hbm, wd_hbm,
    rg_hbm, rt_hbm, gg_hbm, ug_hbm, hid_hbm, out_hbm,
    bg, bt, cg, ct, part, og, tok, sg, su, wg, wu, wd, acc, gg, ug, ggt, ugt, hid, res,
    rp1d, rp1b, rq1d, rq1b, rp2d, rp2b, rq2d, rq2b,
    ssem, rsem, lsem,
):
    width = bg.shape[-1]
    half_w = width // 2
    hidden_n = sg.shape[0]
    pcols, qcols = pl.ds(0, half_w), pl.ds(half_w, half_w)

    e = lax.axis_index("expert")
    y, x, z = e // 8, (e // 2) % 4, e % 2
    a = y // 2
    b = 1 - a
    p = (y + a) % 2
    q = 1 - p
    w = 1 - z
    xp, xm, xo = (x + 1) % 4, (x + 3) % 4, (x + 2) % 4

    def dev(y_, x_, z_):
        return (y_ * 4 + x_) * 2 + z_

    y_dev = dev(2 * a + 1 - y % 2, x, z)
    z_dev = dev(y, x, w)
    xp_dev = dev(y, xp, z)
    xm_dev = dev(y, xm, z)
    c_dev = dev(3 - y, x, z)

    local = []

    def fetch(src, dst):
        c = pltpu.make_async_copy(src, dst, lsem.at[len(local)])
        c.start()
        local.append(c)
        return c

    og_in = fetch(og_hbm, og)
    tok_in = fetch(tok_hbm, tok)
    sg_in = fetch(sg_hbm, sg)
    su_in = fetch(su_hbm, su)
    wd_in = fetch(wd_hbm, wd)
    wg_in = fetch(wg_hbm, wg.at[pl.ds(0, hidden_n)])
    wu_in = fetch(wu_hbm, wu.at[pl.ds(0, hidden_n)])

    barrier = pltpu.get_barrier_semaphore()
    for d in (y_dev, z_dev, xp_dev, xm_dev, c_dev):
        pl.semaphore_signal(barrier, 1, device_id={"expert": d}, device_id_type=pl.DeviceIdType.MESH)

    remote = []

    def send(src, dst, to):
        i = len(remote)
        c = pltpu.make_async_remote_copy(
            src_ref=src, dst_ref=dst, send_sem=ssem.at[i], recv_sem=rsem.at[i],
            device_id={"expert": to}, device_id_type=pl.DeviceIdType.MESH,
        )
        c.start()
        remote.append(c)
        return c

    tokens_n = og.shape[0]
    rows32 = lax.broadcasted_iota(jnp.int32, (2 * CAP, tokens_n), 0)
    pick = jnp.zeros((2 * CAP, tokens_n), jnp.float32)
    scaled = jnp.zeros((2 * CAP, tokens_n), jnp.float32)
    for k in range(2):
        chosen = ids_ref[k:k + 1, :]
        base = jnp.where(chosen == a, 0, jnp.where(chosen == b, CAP, -CAP * CAP))
        hit = rows32 == base + slots_ref[k:k + 1, :]
        weight = gates_ref[k:k + 1, :].astype(jnp.float32) * (1.0 / 256.0)
        pick += jnp.where(hit, 1.0, 0.0)
        scaled += jnp.where(hit, weight, 0.0)
    pick = pick.astype(jnp.bfloat16)
    scaled = scaled.astype(jnp.bfloat16)

    def place(sel, src, buf, other):
        step = 1024
        for c in range(0, width, step):
            rows = jnp.dot(sel, src[:, c:c + step], preferred_element_type=jnp.float32)
            rows = rows.astype(jnp.bfloat16)
            buf[p, a, x, z, :, c:c + step] = rows[:CAP]
            other[:, c:c + step] = rows[CAP:]

    og_in.wait()
    place(scaled, og, bg, cg)
    pl.semaphore_wait(barrier, 5)

    class Gather:
        def __init__(self, buf, other):
            self.buf, self.other = buf, other

        def own(self):
            buf = self.buf
            self.cross = send(self.other, buf.at[p, a, x, z], c_dev)
            self.one_a = self.one(a)

        def one(self, m):
            sp = self.buf.at[p, m, x, z, :, pcols]
            sq = self.buf.at[p, m, x, z, :, qcols]
            return (
                send(sp, sp, y_dev), send(sp, sp, z_dev),
                send(sq, sq, xp_dev), send(sq, sq, xm_dev),
            )

        def crossed(self):
            self.cross.wait_recv()
            self.one_b = self.one(b)

        def fwd1_a(self):
            for c in self.one_a:
                c.wait_recv()
            s1 = self.buf.at[q, a, x, z, :, pcols]
            s2 = self.buf.at[p, a, xm, z, :, qcols]
            self.f1a = (send(s1, s1, z_dev), send(s2, s2, xp_dev))

        def fwd1_b(self):
            for c in self.one_b:
                c.wait_recv()
            s1 = self.buf.at[p, b, x, w, :, pcols]
            s2 = self.buf.at[p, b, xp, z, :, qcols]
            self.f1b = (send(s1, s1, y_dev), send(s2, s2, xm_dev))

        def two(self, m):
            sp = self.buf.at[:, m, x, :, :, pcols]
            sq = self.buf.at[p, m, :, z, :, qcols]
            return (
                send(sp, sp, xp_dev), send(sp, sp, xm_dev),
                send(sq, sq, y_dev), send(sq, sq, z_dev),
            )

        def two_a(self):
            for c in self.f1a:
                c.wait_recv()
            self.t_a = self.two(a)

        def two_b(self):
            for c in self.f1b:
                c.wait_recv()
            self.t_b = self.two(b)

        def fwd2_a(self):
            for c in self.t_a:
                c.wait_recv()
            s1 = self.buf.at[:, a, xm, :, :, pcols]
            s2 = self.buf.at[q, a, :, z, :, qcols]
            self.f2a = (send(s1, s1, xp_dev), send(s2, s2, z_dev))

        def fwd2_b(self):
            for c in self.t_b:
                c.wait_recv()
            s1 = self.buf.at[:, b, xp, :, :, pcols]
            s2 = self.buf.at[p, b, :, w, :, qcols]
            self.f2b = (send(s1, s1, xm_dev), send(s2, s2, y_dev))

        def done(self):
            for c in self.f2a + self.f2b:
                c.wait_recv()

    g = Gather(bg, cg)
    t = Gather(bt, ct)
    g.own()
    tok_in.wait()
    place(pick, tok, bt, ct)
    t.own()
    g.crossed()
    g.fwd1_a()
    t.crossed()
    t.fwd1_a()
    g.fwd1_b()
    g.two_a()
    t.fwd1_b()
    g.two_b()

    sg_in.wait()
    su_in.wait()
    for chunk in range(4):
        src = slice(128 * Y_OF_CHUNK[chunk], 128 * Y_OF_CHUNK[chunk] + 128)
        gate = sg[:, src].astype(jnp.float32)
        up = su[:, src].astype(jnp.float32)
        sig = 1.0 / (1.0 + jnp.exp(-gate))
        hid[:, 128 * chunk:128 * chunk + 128] = (gate * sig * up).astype(jnp.bfloat16)
    hid_out = fetch(hid, hid_hbm)
    acc[...] = jnp.zeros_like(acc)
    pad = wg.shape[0] - hidden_n
    wg[hidden_n:, :] = jnp.zeros((pad, width), wg.dtype)
    wu[hidden_n:, :] = jnp.zeros((pad, width), wu.dtype)

    g.fwd2_a()
    t.two_a()
    wd_in.wait()
    g.fwd2_b()
    t.two_b()
    g.done()
    rg_out = fetch(bg, rg_hbm)

    k_step = width // 4
    for c in range(2):
        cols = slice(256 * c, 256 * c + 256)

        def hid_step(k, _, c=c, cols=cols):
            ks = pl.ds(pl.multiple_of(k * k_step, 128), k_step)
            rows = bg[c, :, :, :, :, ks].reshape(256, k_step)
            acc[:, cols] += lax.dot_general(
                wd[:, ks], rows, (((1,), (1,)), ((), ())), preferred_element_type=jnp.float32
            )
            return 0

        lax.fori_loop(0, 4, hid_step, 0)

    t.fwd2_a()
    for chunk in range(4):
        src = slice(128 * Y_OF_CHUNK[chunk], 128 * Y_OF_CHUNK[chunk] + 128)
        dst = slice(128 * chunk, 128 * chunk + 128)
        gate = sg[:, src].astype(jnp.float32)
        up = su[:, src].astype(jnp.float32)
        sig = 1.0 / (1.0 + jnp.exp(-gate))
        down = acc[:, dst]
        g_gate = down * up * sig * (1.0 + gate * (1.0 - sig))
        g_up = down * (gate * sig)
        ggt[:, dst] = g_gate.astype(jnp.bfloat16)
        ugt[:, dst] = g_up.astype(jnp.bfloat16)
        zeros = jnp.zeros((pad, 128), jnp.float32)
        gg[dst, :] = jnp.concatenate([g_gate, zeros], axis=0).T.astype(jnp.bfloat16)
        ug[dst, :] = jnp.concatenate([g_up, zeros], axis=0).T.astype(jnp.bfloat16)
    gg_out = fetch(ggt, gg_hbm)
    ug_out = fetch(ugt, ug_hbm)

    n_step = 512

    def parts(first):
        for c in range(2):

            def part_step(n, _, c=c):
                ns = pl.ds(pl.multiple_of(first + n * n_step, 128), n_step)
                rows = slice(256 * c, 256 * c + 256)
                o = jnp.dot(gg[rows, :], wg[:, ns], preferred_element_type=jnp.float32)
                o += jnp.dot(ug[rows, :], wu[:, ns], preferred_element_type=jnp.float32)
                part[c, :, :, :, :, ns] = o.astype(jnp.bfloat16).reshape(2, 4, 2, CAP, n_step)
                return 0

            lax.fori_loop(0, half_w // n_step, part_step, 0)

    f32 = jnp.float32
    bf = jnp.bfloat16

    wg_in.wait()
    wu_in.wait()
    parts(0)
    p1 = (
        send(part.at[:, a, xo, :, :, pcols], rp1d.at[0], xp_dev),
        send(part.at[:, b, xo, :, :, pcols], rp1d.at[1], xm_dev),
    )
    p1r = (
        send(part.at[:, b, xp, :, :, pcols], rp1b.at[0, 1], xp_dev),
        send(part.at[:, a, xm, :, :, pcols], rp1b.at[1, 0], xm_dev),
    )
    t.fwd2_b()
    parts(half_w)
    q1 = (
        send(part.at[q, a, :, w, :, qcols], rq1d.at[0], y_dev),
        send(part.at[q, b, :, w, :, qcols], rq1d.at[1], z_dev),
    )
    q1r = (
        send(part.at[p, b, :, w, :, qcols], rq1b.at[0, 1], z_dev),
        send(part.at[q, a, :, z, :, qcols], rq1b.at[1, 0], y_dev),
    )

    p1[0].wait_recv()
    for i in range(2):
        for j in range(2):
            part[i, a, xp, j, :, pcols] = (
                part[i, a, xp, j, :, pcols].astype(f32) + rp1d[0, i, j].astype(f32)
            ).astype(bf)
    p1s0 = send(part.at[:, a, xp, :, :, pcols], rp1b.at[0, 0], xp_dev)
    p1[1].wait_recv()
    for i in range(2):
        for j in range(2):
            part[i, b, xm, j, :, pcols] = (
                part[i, b, xm, j, :, pcols].astype(f32) + rp1d[1, i, j].astype(f32)
            ).astype(bf)
    p1s1 = send(part.at[:, b, xm, :, :, pcols], rp1b.at[1, 1], xm_dev)

    q1[0].wait_recv()
    for i in range(4):
        part[p, a, i, w, :, qcols] = (
            part[p, a, i, w, :, qcols].astype(f32) + rq1d[0, i].astype(f32)
        ).astype(bf)
    q1s0 = send(part.at[p, a, :, w, :, qcols], rq1b.at[0, 0], z_dev)
    q1[1].wait_recv()
    for i in range(4):
        part[q, b, i, z, :, qcols] = (
            part[q, b, i, z, :, qcols].astype(f32) + rq1d[1, i].astype(f32)
        ).astype(bf)
    q1s1 = send(part.at[q, b, :, z, :, qcols], rq1b.at[1, 1], y_dev)

    t.done()
    rt_out = fetch(bt, rt_hbm)

    for c in p1r + (p1s0, p1s1):
        c.wait_recv()
    for i in range(2):
        for s, m in ((0, a), (1, b)):
            for j in range(2):
                part[i, m, x, j, :, pcols] = (
                    part[i, m, x, j, :, pcols].astype(f32)
                    + rp1b[0, s, i, j].astype(f32) + rp1b[1, s, i, j].astype(f32)
                ).astype(bf)
    p2 = (
        send(part.at[q, a, x, w, :, pcols], rp2d.at[0], y_dev),
        send(part.at[q, b, x, w, :, pcols], rp2d.at[1], z_dev),
    )
    p2r = (
        send(part.at[p, b, x, w, :, pcols], rp2b.at[0, 1], z_dev),
        send(part.at[q, a, x, z, :, pcols], rp2b.at[1, 0], y_dev),
    )
    for c in q1r + (q1s0, q1s1):
        c.wait_recv()
    for i in range(4):
        for s, m in ((0, a), (1, b)):
            part[p, m, i, z, :, qcols] = (
                part[p, m, i, z, :, qcols].astype(f32)
                + rq1b[0, s, i].astype(f32) + rq1b[1, s, i].astype(f32)
            ).astype(bf)
    q2 = (
        send(part.at[p, a, xo, z, :, qcols], rq2d.at[0], xp_dev),
        send(part.at[p, b, xo, z, :, qcols], rq2d.at[1], xm_dev),
    )
    q2r = (
        send(part.at[p, b, xp, z, :, qcols], rq2b.at[0, 1], xp_dev),
        send(part.at[p, a, xm, z, :, qcols], rq2b.at[1, 0], xm_dev),
    )

    p2[0].wait_recv()
    part[p, a, x, w, :, pcols] = (
        part[p, a, x, w, :, pcols].astype(f32) + rp2d[0].astype(f32)
    ).astype(bf)
    p2s0 = send(part.at[p, a, x, w, :, pcols], rp2b.at[0, 0], z_dev)
    p2[1].wait_recv()
    part[q, b, x, z, :, pcols] = (
        part[q, b, x, z, :, pcols].astype(f32) + rp2d[1].astype(f32)
    ).astype(bf)
    p2s1 = send(part.at[q, b, x, z, :, pcols], rp2b.at[1, 1], y_dev)
    q2[0].wait_recv()
    part[p, a, xp, z, :, qcols] = (
        part[p, a, xp, z, :, qcols].astype(f32) + rq2d[0].astype(f32)
    ).astype(bf)
    q2s0 = send(part.at[p, a, xp, z, :, qcols], rq2b.at[0, 0], xp_dev)
    q2[1].wait_recv()
    part[p, b, xm, z, :, qcols] = (
        part[p, b, xm, z, :, qcols].astype(f32) + rq2d[1].astype(f32)
    ).astype(bf)
    q2s1 = send(part.at[p, b, xm, z, :, qcols], rq2b.at[1, 1], xm_dev)

    for c in p2r + (p2s0, p2s1):
        c.wait_recv()
    for s, m in ((0, a), (1, b)):
        res[s, :, pcols] = (
            part[p, m, x, z, :, pcols].astype(f32)
            + rp2b[0, s].astype(f32) + rp2b[1, s].astype(f32)
        ).astype(bf)
    for c in q2r + (q2s0, q2s1):
        c.wait_recv()
    for s, m in ((0, a), (1, b)):
        res[s, :, qcols] = (
            part[p, m, x, z, :, qcols].astype(f32)
            + rq2b[0, s].astype(f32) + rq2b[1, s].astype(f32)
        ).astype(bf)
    res_out = fetch(res, out_hbm)

    for c in remote:
        c.wait_send()
    for c in (hid_out, rg_out, gg_out, ug_out, rt_out, res_out):
        c.wait()


def exchange(ids, slots, gates, tok, og, sg, su, wg, wu, wd):
    width = tok.shape[-1]
    tokens_n = tok.shape[0]
    hidden_n = sg.shape[0]
    half = width // 2
    bf = jnp.bfloat16
    rows_shape = (2, 2, 4, 2, CAP, width)
    padded = -(-hidden_n // 128) * 128
    any_spec = pl.BlockSpec(memory_space=pl.ANY)
    vmem_spec = pl.BlockSpec(memory_space=pltpu.VMEM)
    vm = pltpu.VMEM
    return pl.pallas_call(
        kernel,
        name="exchange",
        out_shape=(
            jax.ShapeDtypeStruct(rows_shape, bf),
            jax.ShapeDtypeStruct(rows_shape, bf),
            jax.ShapeDtypeStruct((hidden_n, ROWS), bf),
            jax.ShapeDtypeStruct((hidden_n, ROWS), bf),
            jax.ShapeDtypeStruct((hidden_n, ROWS), bf),
            jax.ShapeDtypeStruct((2, CAP, width), bf),
        ),
        in_specs=[vmem_spec] * 3 + [any_spec] * 7,
        out_specs=[any_spec] * 6,
        scratch_shapes=[
            vm(rows_shape, bf), vm(rows_shape, bf),
            vm((CAP, width), bf), vm((CAP, width), bf),
            vm(rows_shape, bf),
            vm((tokens_n, width), bf), vm((tokens_n, width), bf),
            vm((hidden_n, ROWS), bf), vm((hidden_n, ROWS), bf),
            vm((padded, width), bf), vm((padded, width), bf), vm((hidden_n, width), bf),
            vm((hidden_n, ROWS), jnp.float32),
            vm((ROWS, padded), bf), vm((ROWS, padded), bf),
            vm((hidden_n, ROWS), bf), vm((hidden_n, ROWS), bf), vm((hidden_n, ROWS), bf),
            vm((2, CAP, width), bf),
            vm((2, 2, 2, CAP, half), bf), vm((2, 2, 2, 2, CAP, half), bf),
            vm((2, 4, CAP, half), bf), vm((2, 2, 4, CAP, half), bf),
            vm((2, CAP, half), bf), vm((2, 2, CAP, half), bf),
            vm((2, CAP, half), bf), vm((2, 2, CAP, half), bf),
            pltpu.SemaphoreType.DMA((COPIES,)), pltpu.SemaphoreType.DMA((COPIES,)),
            pltpu.SemaphoreType.DMA((16,)),
        ],
        compiler_params=pltpu.CompilerParams(
            collective_id=0, has_side_effects=True, vmem_limit_bytes=56 << 20
        ),
        cost_estimate=pl.CostEstimate(
            flops=6 * ROWS * hidden_n * width, transcendentals=2 * ROWS * hidden_n,
            bytes_accessed=40 << 20,
        ),
    )(ids, slots, gates, tok, og, sg, su, wg, wu, wd)


def shards(
    tokens, out_grad, expert_ids, slot_ids, gate_int, saved_gate, saved_up, w_gate, w_up, w_down
):
    width = tokens.shape[-1]
    sections = lax.axis_size("section")
    devices = lax.axis_size("expert")
    ids, slots, gates = expert_ids[0].T, slot_ids[0].T, gate_int[0].T

    back = [(s * devices + i, (s - 1) * devices + i) for s in range(1, sections) for i in range(devices)]
    back_cross = [
        (s * devices + i, (s - 1) * devices + (3 - i // 8) * 8 + i % 8)
        for s in range(1, sections) for i in range(devices)
    ]
    axes = ("section", "expert")
    table = lax.ppermute(jnp.stack([ids, slots]), axes, back)

    rows_grad, rows_in, gate_t, up_t, hidden_t, summed = exchange(
        ids, slots, gates, tokens[0], out_grad[0], saved_gate[0].T, saved_up[0].T,
        w_gate[0].T, w_up[0].T, w_down[0],
    )
    own = lax.ppermute(summed[0], axes, back)
    other = lax.ppermute(summed[1], axes, back_cross)

    rows_grad = rows_grad.reshape(ROWS, width)
    rows_in = rows_in.reshape(ROWS, width)

    def product(left, right):
        return jnp.dot(left, right, preferred_element_type=jnp.float32).astype(jnp.bfloat16)

    grad_down = product(hidden_t, rows_grad)
    grad_gate = product(gate_t, rows_in).T
    grad_up = product(up_t, rows_in).T

    mine = lax.axis_index("expert") // (devices // E_WIN)
    slot = lax.iota(jnp.int32, CAP)

    def taken(expert):
        hit = jnp.logical_and(table[0][:, :, None] == expert, table[1][:, :, None] == slot)
        return jnp.any(hit, axis=0)

    select = jnp.concatenate([taken(mine), taken(1 - mine)], axis=1).astype(jnp.bfloat16)
    arriving = jnp.dot(
        select, jnp.concatenate([own, other], axis=0), preferred_element_type=jnp.float32
    ).astype(jnp.bfloat16)
    return (arriving[None], grad_gate[None], grad_up[None], grad_down[None])


def solution(mesh):
    row = P("section", "expert", None)
    col = P("section", None, "expert")
    return jax.shard_map(
        shards,
        mesh=mesh,
        in_specs=(row,) * 5 + (col,) * 4 + (row,),
        out_specs=(row, col, col, row),
        check_vma=False,
    )
```

```python
import jax
import jax.numpy as jnp
from jax import lax
from jax.experimental import pallas as pl
from jax.experimental.pallas import tpu as pltpu
from jax.sharding import PartitionSpec as P

CAP = 16
ROWS = 512
Y_OF_CHUNK = (0, 3, 1, 2)
COPIES = 112
PIECES = 2
VMEM_MIB = 40


def kernel(
    ids_hbm, slots_hbm, gates_hbm, tok_hbm, og_hbm, sg_hbm, su_hbm, wg_hbm, wu_hbm, wd_hbm,
    arr_hbm, dg_hbm, du_hbm, dd_hbm,
    bg, bt, cg, ct, part, og, tok, sg, su, wg, wu, wd, acc, fa, fb, gg, ug, ggt, ugt, hid,
    res, fin, pick_out, pick_in, ids_ref, slots_ref, gates_ref,
    rp1d, rp1b, rq1d, rq1b, rp2d, rp2b, rq2d, rq2b,
    ssem, rsem, lsem,
):
    f32 = jnp.float32
    bf = jnp.bfloat16
    width = bg.shape[-1]
    half_w = width // 2
    piece = half_w // PIECES
    hidden_n = sg.shape[0]
    pad = wg.shape[0] - hidden_n
    pcols, qcols = pl.ds(0, half_w), pl.ds(half_w, half_w)

    sections = lax.axis_size("section")
    sec = lax.axis_index("section")
    e = lax.axis_index("expert")
    y, x, z = e // 8, (e // 2) % 4, e % 2
    a = y // 2
    b = 1 - a
    p = (y + a) % 2
    q = 1 - p
    w = 1 - z
    xp, xm, xo = (x + 1) % 4, (x + 3) % 4, (x + 2) % 4
    before, after = (sec + sections - 1) % sections, (sec + 1) % sections

    def dev(y_, x_, z_):
        return (y_ * 4 + x_) * 2 + z_

    cross = dev(3 - y, x, z)
    y_dev = (sec, dev(2 * a + 1 - y % 2, x, z))
    z_dev = (sec, dev(y, x, w))
    xp_dev = (sec, dev(y, xp, z))
    xm_dev = (sec, dev(y, xm, z))
    c_dev = (sec, cross)

    local = []

    def fetch(src, dst):
        c = pltpu.make_async_copy(src, dst, lsem.at[len(local)])
        c.start()
        local.append(c)
        return c

    small_in = (fetch(ids_hbm, ids_ref), fetch(slots_hbm, slots_ref), fetch(gates_hbm, gates_ref))
    og_in = fetch(og_hbm, og)
    tok_in = fetch(tok_hbm, tok)
    sg_in = fetch(sg_hbm, sg)
    su_in = fetch(su_hbm, su)
    wd_in = fetch(wd_hbm, wd.at[pl.ds(0, hidden_n)])
    wg_in = fetch(wg_hbm, wg.at[pl.ds(0, hidden_n)])
    wu_in = fetch(wu_hbm, wu.at[pl.ds(0, hidden_n)])

    barrier = pltpu.get_barrier_semaphore()
    for d in (y_dev, z_dev, xp_dev, xm_dev, c_dev, (after, e), (after, cross)):
        pl.semaphore_signal(barrier, 1, device_id=d, device_id_type=pl.DeviceIdType.MESH)

    remote = []

    def send(src, dst, to):
        i = len(remote)
        c = pltpu.make_async_remote_copy(
            src_ref=src, dst_ref=dst, send_sem=ssem.at[i], recv_sem=rsem.at[i],
            device_id=to, device_id_type=pl.DeviceIdType.MESH,
        )
        c.start()
        remote.append(c)
        return c

    def arrived(copies):
        for c in copies:
            c.wait_recv()

    for c in small_in:
        c.wait()
    tokens_n = og.shape[0]
    rows32 = lax.broadcasted_iota(jnp.int32, (2 * CAP, tokens_n), 0)
    pick = jnp.zeros((2 * CAP, tokens_n), f32)
    scaled = jnp.zeros((2 * CAP, tokens_n), f32)
    for k in range(2):
        chosen = ids_ref[k:k + 1, :]
        base = jnp.where(chosen == a, 0, jnp.where(chosen == b, CAP, -CAP * CAP))
        hit = rows32 == base + slots_ref[k:k + 1, :]
        weight = gates_ref[k:k + 1, :].astype(f32) * (1.0 / 256.0)
        pick += jnp.where(hit, 1.0, 0.0)
        scaled += jnp.where(hit, weight, 0.0)
    pick = pick.astype(bf)
    scaled = scaled.astype(bf)
    pick_out[...] = pick

    def place(sel, src, buf, other):
        step = 1024
        for c in range(0, width, step):
            rows = jnp.dot(sel, src[:, c:c + step], preferred_element_type=f32)
            rows = rows.astype(bf)
            buf[p, a, x, z, :, c:c + step] = rows[:CAP]
            other[:, c:c + step] = rows[CAP:]

    og_in.wait()
    place(scaled, og, bg, cg)
    pl.semaphore_wait(barrier, 7)

    class Gather:
        def __init__(self, buf, other):
            self.buf, self.other = buf, other

        def own(self):
            buf = self.buf
            self.cross = send(self.other, buf.at[p, a, x, z], c_dev)
            self.one_a = self.one(a)

        def one(self, m):
            sp = self.buf.at[p, m, x, z, :, pcols]
            sq = self.buf.at[p, m, x, z, :, qcols]
            return (
                send(sp, sp, y_dev), send(sp, sp, z_dev),
                send(sq, sq, xp_dev), send(sq, sq, xm_dev),
            )

        def crossed(self):
            self.cross.wait_recv()
            self.one_b = self.one(b)

        def fwd1_a(self):
            arrived(self.one_a)
            s1 = self.buf.at[q, a, x, z, :, pcols]
            s2 = self.buf.at[p, a, xm, z, :, qcols]
            self.f1a = (send(s1, s1, z_dev), send(s2, s2, xp_dev))

        def fwd1_b(self):
            arrived(self.one_b)
            s1 = self.buf.at[p, b, x, w, :, pcols]
            s2 = self.buf.at[p, b, xp, z, :, qcols]
            self.f1b = (send(s1, s1, y_dev), send(s2, s2, xm_dev))

        def two(self, m):
            sp = self.buf.at[:, m, x, :, :, pcols]
            sq = self.buf.at[p, m, :, z, :, qcols]
            return (
                send(sp, sp, xp_dev), send(sp, sp, xm_dev),
                send(sq, sq, y_dev), send(sq, sq, z_dev),
            )

        def two_a(self):
            arrived(self.f1a)
            self.t_a = self.two(a)

        def two_b(self):
            arrived(self.f1b)
            self.t_b = self.two(b)

        def fwd2_a(self):
            arrived(self.t_a)
            s1 = self.buf.at[:, a, xm, :, :, pcols]
            s2 = self.buf.at[q, a, :, z, :, qcols]
            self.f2a = (send(s1, s1, xp_dev), send(s2, s2, z_dev))

        def fwd2_b(self):
            arrived(self.t_b)
            s1 = self.buf.at[:, b, xp, :, :, pcols]
            s2 = self.buf.at[p, b, :, w, :, qcols]
            self.f2b = (send(s1, s1, xm_dev), send(s2, s2, y_dev))

        def done(self):
            arrived(self.f2a + self.f2b)

    g = Gather(bg, cg)
    t = Gather(bt, ct)
    g.own()
    tok_in.wait()
    place(pick, tok, bt, ct)
    t.own()
    g.crossed()
    g.fwd1_a()
    t.crossed()
    t.fwd1_a()
    g.fwd1_b()
    g.two_a()
    t.fwd1_b()
    g.two_b()

    pick_sent = send(pick_out, pick_in, (before, e))

    sg_in.wait()
    su_in.wait()
    zeros = jnp.zeros((pad, 128), f32)
    for chunk in range(4):
        src = slice(128 * Y_OF_CHUNK[chunk], 128 * Y_OF_CHUNK[chunk] + 128)
        dst = slice(128 * chunk, 128 * chunk + 128)
        gate = sg[:, src].astype(f32)
        up = su[:, src].astype(f32)
        sig = 1.0 / (1.0 + jnp.exp(-gate))
        active = gate * sig
        hid[:, dst] = (active * up).astype(bf)
        slope = up * sig * (1.0 + gate * (1.0 - sig))
        fa[dst, :] = jnp.concatenate([slope, zeros], axis=0).T
        fb[dst, :] = jnp.concatenate([active, zeros], axis=0).T
    acc[...] = jnp.zeros_like(acc)
    for buf in (wd, wg, wu):
        buf[hidden_n:, :] = jnp.zeros((pad, width), bf)

    g.fwd2_a()
    t.two_a()
    wd_in.wait()
    g.fwd2_b()
    t.two_b()
    g.done()

    k_step = width // 4

    def hid_step(k, _):
        ks = pl.ds(pl.multiple_of(k * k_step, 128), k_step)
        rows = bg[:, :, :, :, :, ks].reshape(ROWS, k_step)
        acc[...] += lax.dot_general(
            rows, wd[:, ks], (((1,), (1,)), ((), ())), preferred_element_type=f32
        )
        return 0

    lax.fori_loop(0, 4, hid_step, 0)
    gg[...] = (acc[...] * fa[...]).astype(bf)
    ug[...] = (acc[...] * fb[...]).astype(bf)

    n_step = 512

    def parts(first):

        def part_step(n, _):
            ns = pl.ds(pl.multiple_of(first + n * n_step, 128), n_step)
            o = jnp.dot(gg[...], wg[:, ns], preferred_element_type=f32)
            o += jnp.dot(ug[...], wu[:, ns], preferred_element_type=f32)
            part[:, :, :, :, :, ns] = o.astype(bf).reshape(2, 2, 4, 2, CAP, n_step)
            return 0

        lax.fori_loop(0, piece // n_step, part_step, 0)

    def plus(dst, index, *others):
        total = dst[index].astype(f32)
        for o in others:
            total += o.astype(f32)
        dst[index] = total.astype(bf)

    def to_before(c):
        self_cols = c
        return (
            send(res.at[0, :, self_cols], fin.at[0, :, self_cols], (before, e)),
            send(res.at[1, :, self_cols], fin.at[1, :, self_cols], (before, cross)),
        )

    class ScatterP:
        def __init__(self, k):
            self.k, self.first = k, k * piece
            self.c = pl.ds(self.first, piece)

        def start(self):
            k, c = self.k, self.c
            parts(self.first)
            self.d1 = (
                send(part.at[:, a, xo, :, :, c], rp1d.at[k, 0], xp_dev),
                send(part.at[:, b, xo, :, :, c], rp1d.at[k, 1], xm_dev),
            )
            self.b1 = (
                send(part.at[:, b, xp, :, :, c], rp1b.at[k, 0, 1], xp_dev),
                send(part.at[:, a, xm, :, :, c], rp1b.at[k, 1, 0], xm_dev),
            )

        def diag1(self):
            k, c = self.k, self.c
            arrived(self.d1[:1])
            for i in range(2):
                for j in range(2):
                    plus(part, (i, a, xp, j, slice(None), c), rp1d[k, 0, i, j])
            s0 = send(part.at[:, a, xp, :, :, c], rp1b.at[k, 0, 0], xp_dev)
            arrived(self.d1[1:])
            for i in range(2):
                for j in range(2):
                    plus(part, (i, b, xm, j, slice(None), c), rp1d[k, 1, i, j])
            s1 = send(part.at[:, b, xm, :, :, c], rp1b.at[k, 1, 1], xm_dev)
            self.b1 += (s0, s1)

        def sum1(self):
            k, c = self.k, self.c
            arrived(self.b1)
            for i in range(2):
                for s, m in ((0, a), (1, b)):
                    for j in range(2):
                        plus(part, (i, m, x, j, slice(None), c), rp1b[k, 0, s, i, j], rp1b[k, 1, s, i, j])
            self.d2 = (
                send(part.at[q, a, x, w, :, c], rp2d.at[k, 0], y_dev),
                send(part.at[q, b, x, w, :, c], rp2d.at[k, 1], z_dev),
            )
            self.b2 = (
                send(part.at[p, b, x, w, :, c], rp2b.at[k, 0, 1], z_dev),
                send(part.at[q, a, x, z, :, c], rp2b.at[k, 1, 0], y_dev),
            )

        def diag2(self):
            k, c = self.k, self.c
            arrived(self.d2[:1])
            plus(part, (p, a, x, w, slice(None), c), rp2d[k, 0])
            s0 = send(part.at[p, a, x, w, :, c], rp2b.at[k, 0, 0], z_dev)
            arrived(self.d2[1:])
            plus(part, (q, b, x, z, slice(None), c), rp2d[k, 1])
            s1 = send(part.at[q, b, x, z, :, c], rp2b.at[k, 1, 1], y_dev)
            self.b2 += (s0, s1)

        def last(self):
            k, c = self.k, self.c
            arrived(self.b2)
            for s, m in ((0, a), (1, b)):
                res[s, :, c] = (
                    part[p, m, x, z, :, c].astype(f32)
                    + rp2b[k, 0, s].astype(f32) + rp2b[k, 1, s].astype(f32)
                ).astype(bf)
            self.out = to_before(c)

    class ScatterQ:
        def __init__(self, k):
            self.k, self.first = k, half_w + k * piece
            self.c = pl.ds(self.first, piece)

        def start(self):
            k, c = self.k, self.c
            parts(self.first)
            self.d1 = (
                send(part.at[q, a, :, w, :, c], rq1d.at[k, 0], y_dev),
                send(part.at[q, b, :, w, :, c], rq1d.at[k, 1], z_dev),
            )
            self.b1 = (
                send(part.at[p, b, :, w, :, c], rq1b.at[k, 0, 1], z_dev),
                send(part.at[q, a, :, z, :, c], rq1b.at[k, 1, 0], y_dev),
            )

        def diag1(self):
            k, c = self.k, self.c
            arrived(self.d1[:1])
            for i in range(4):
                plus(part, (p, a, i, w, slice(None), c), rq1d[k, 0, i])
            s0 = send(part.at[p, a, :, w, :, c], rq1b.at[k, 0, 0], z_dev)
            arrived(self.d1[1:])
            for i in range(4):
                plus(part, (q, b, i, z, slice(None), c), rq1d[k, 1, i])
            s1 = send(part.at[q, b, :, z, :, c], rq1b.at[k, 1, 1], y_dev)
            self.b1 += (s0, s1)

        def sum1(self):
            k, c = self.k, self.c
            arrived(self.b1)
            for i in range(4):
                for s, m in ((0, a), (1, b)):
                    plus(part, (p, m, i, z, slice(None), c), rq1b[k, 0, s, i], rq1b[k, 1, s, i])
            self.d2 = (
                send(part.at[p, a, xo, z, :, c], rq2d.at[k, 0], xp_dev),
                send(part.at[p, b, xo, z, :, c], rq2d.at[k, 1], xm_dev),
            )
            self.b2 = (
                send(part.at[p, b, xp, z, :, c], rq2b.at[k, 0, 1], xp_dev),
                send(part.at[p, a, xm, z, :, c], rq2b.at[k, 1, 0], xm_dev),
            )

        def diag2(self):
            k, c = self.k, self.c
            arrived(self.d2[:1])
            plus(part, (p, a, xp, z, slice(None), c), rq2d[k, 0])
            s0 = send(part.at[p, a, xp, z, :, c], rq2b.at[k, 0, 0], xp_dev)
            arrived(self.d2[1:])
            plus(part, (p, b, xm, z, slice(None), c), rq2d[k, 1])
            s1 = send(part.at[p, b, xm, z, :, c], rq2b.at[k, 1, 1], xm_dev)
            self.b2 += (s0, s1)

        def last(self):
            k, c = self.k, self.c
            arrived(self.b2)
            for s, m in ((0, a), (1, b)):
                res[s, :, c] = (
                    part[p, m, x, z, :, c].astype(f32)
                    + rq2b[k, 0, s].astype(f32) + rq2b[k, 1, s].astype(f32)
                ).astype(bf)
            self.out = to_before(c)

    def weight_grad(left, rows, out):

        def grad_step(n, _):
            ns = pl.ds(pl.multiple_of(n * n_step, 128), n_step)
            right = rows[:, :, :, :, :, ns].reshape(ROWS, n_step)
            out[pl.ds(0, hidden_n), ns] = jnp.dot(left[...], right, preferred_element_type=f32).astype(bf)
            return 0

        lax.fori_loop(0, width // n_step, grad_step, 0)

    p0, p1 = ScatterP(0), ScatterP(1)
    q0, q1 = ScatterQ(0), ScatterQ(1)
    wg_in.wait()
    wu_in.wait()
    p0.start()
    q0.start()
    p1.start()
    q1.start()
    t.fwd2_a()
    p0.diag1()
    q0.diag1()
    weight_grad(hid, bg, wd)
    dd_out = fetch(wd.at[pl.ds(0, hidden_n)], dd_hbm)
    p1.diag1()
    q1.diag1()
    t.fwd2_b()
    p0.sum1()
    q0.sum1()
    for chunk in range(4):
        dst = slice(128 * chunk, 128 * chunk + 128)
        ggt[:, dst] = gg[dst, :].astype(f32).T[:hidden_n].astype(bf)
        ugt[:, dst] = ug[dst, :].astype(f32).T[:hidden_n].astype(bf)
    p1.sum1()
    q1.sum1()
    p0.diag2()
    q0.diag2()
    p1.diag2()
    q1.diag2()
    p0.last()
    q0.last()
    p1.last()
    q1.last()
    t.done()
    weight_grad(ggt, bt, wg)
    dg_out = fetch(wg.at[pl.ds(0, hidden_n)], dg_hbm)
    weight_grad(ugt, bt, wu)
    du_out = fetch(wu.at[pl.ds(0, hidden_n)], du_hbm)

    pick_sent.wait_recv()
    arrived(p0.out + p1.out + q0.out + q1.out)
    took = jnp.where(sec == sections - 1, 0.0, pick_in[...].astype(f32)).T.astype(bf)
    step = 1024
    for c in range(0, width, step):
        rows = fin[:, :, c:c + step].reshape(2 * CAP, step)
        tok[:, c:c + step] = jnp.dot(took, rows, preferred_element_type=f32).astype(bf)
    arr_out = fetch(tok, arr_hbm)

    for c in remote:
        c.wait_send()
    for c in (dd_out, dg_out, du_out, arr_out):
        c.wait()


def exchange(ids, slots, gates, tok, og, sg, su, wg, wu, wd):
    width = tok.shape[-1]
    tokens_n = tok.shape[0]
    hidden_n = sg.shape[0]
    piece = width // 2 // PIECES
    f32, bf = jnp.float32, jnp.bfloat16
    rows_shape = (2, 2, 4, 2, CAP, width)
    padded = -(-hidden_n // 128) * 128
    any_spec = pl.BlockSpec(memory_space=pl.ANY)
    vm = pltpu.VMEM
    grad = jax.ShapeDtypeStruct((hidden_n, width), bf)
    return pl.pallas_call(
        kernel,
        name="exchange",
        out_shape=(jax.ShapeDtypeStruct((tokens_n, width), bf), grad, grad, grad),
        in_specs=[pl.BlockSpec(memory_space=pltpu.HBM)] * 10,
        out_specs=[any_spec] * 4,
        scratch_shapes=[
            vm(rows_shape, bf), vm(rows_shape, bf),
            vm((CAP, width), bf), vm((CAP, width), bf),
            vm(rows_shape, bf),
            vm((tokens_n, width), bf), vm((tokens_n, width), bf),
            vm((hidden_n, ROWS), bf), vm((hidden_n, ROWS), bf),
            vm((padded, width), bf), vm((padded, width), bf), vm((padded, width), bf),
            vm((ROWS, padded), f32), vm((ROWS, padded), f32), vm((ROWS, padded), f32),
            vm((ROWS, padded), bf), vm((ROWS, padded), bf),
            vm((hidden_n, ROWS), bf), vm((hidden_n, ROWS), bf), vm((hidden_n, ROWS), bf),
            vm((2, CAP, width), bf), vm((2, CAP, width), bf),
            vm((2 * CAP, tokens_n), bf), vm((2 * CAP, tokens_n), bf),
            vm(ids.shape, jnp.int32), vm(ids.shape, jnp.int32), vm(ids.shape, jnp.int32),
            vm((PIECES, 2, 2, 2, CAP, piece), bf), vm((PIECES, 2, 2, 2, 2, CAP, piece), bf),
            vm((PIECES, 2, 4, CAP, piece), bf), vm((PIECES, 2, 2, 4, CAP, piece), bf),
            vm((PIECES, 2, CAP, piece), bf), vm((PIECES, 2, 2, CAP, piece), bf),
            vm((PIECES, 2, CAP, piece), bf), vm((PIECES, 2, 2, CAP, piece), bf),
            pltpu.SemaphoreType.DMA((COPIES,)), pltpu.SemaphoreType.DMA((COPIES,)),
            pltpu.SemaphoreType.DMA((16,)),
        ],
        compiler_params=pltpu.CompilerParams(
            collective_id=0, has_side_effects=True, vmem_limit_bytes=VMEM_MIB << 20
        ),
        cost_estimate=pl.CostEstimate(
            flops=12 * ROWS * hidden_n * width, transcendentals=ROWS * hidden_n,
            bytes_accessed=24 << 20,
        ),
    )(ids, slots, gates, tok, og, sg, su, wg, wu, wd)


def store_kernel(*refs):
    ins, outs, sem = refs[:4], refs[4:8], refs[8]
    copies = []
    for src, dst in zip(ins, outs):
        rows = src.shape[0]
        for first in range(0, rows, rows // 2):
            part = pl.ds(first, rows // 2)
            copies.append(pltpu.make_async_copy(src.at[part], dst.at[part], sem.at[len(copies)]))
            copies[-1].start()
    for c in copies:
        c.wait()


def store(*arrays):
    size = sum(v.size for v in arrays)
    return pl.pallas_call(
        store_kernel,
        name="store",
        out_shape=tuple(jax.ShapeDtypeStruct(v.shape, v.dtype) for v in arrays),
        in_specs=[pl.BlockSpec(memory_space=pl.ANY)] * 4,
        out_specs=[pl.BlockSpec(memory_space=pltpu.HBM)] * 4,
        scratch_shapes=[pltpu.SemaphoreType.DMA((8,))],
        compiler_params=pltpu.CompilerParams(vmem_limit_bytes=1 << 20),
        cost_estimate=pl.CostEstimate(flops=0, transcendentals=0, bytes_accessed=4 * size),
    )(*arrays)


def shards(
    tokens, out_grad, expert_ids, slot_ids, gate_int, saved_gate, saved_up, w_gate, w_up, w_down
):
    arriving, grad_gate, grad_up, grad_down = exchange(
        *[pltpu.with_memory_space_constraint(v, pltpu.HBM) for v in (expert_ids[0].T, slot_ids[0].T, gate_int[0].T, tokens[0], out_grad[0],
        saved_gate[0].T, saved_up[0].T, w_gate[0].T, w_up[0].T, w_down[0])],
    )
    arriving, grad_gate, grad_up, grad_down = store(arriving, grad_gate, grad_up, grad_down)
    return (arriving[None], grad_gate.T[None], grad_up.T[None], grad_down[None])


def solution(mesh):
    row = P("section", "expert", None)
    col = P("section", None, "expert")
    return jax.shard_map(
        shards,
        mesh=mesh,
        in_specs=(row,) * 5 + (col,) * 4 + (row,),
        out_specs=(row, col, col, row),
        check_vma=False,
    )
```

```python
import jax
import jax.numpy as jnp
from jax import lax
from jax.experimental import pallas as pl
from jax.experimental.pallas import tpu as pltpu
from jax.sharding import PartitionSpec as P

CAP = 16
ROWS = 512
Y_OF_CHUNK = (0, 3, 1, 2)
COPIES = 112
PIECES = 2
VMEM_MIB = 40


def kernel(
    ids_hbm, slots_hbm, gates_hbm, tok_hbm, og_hbm, sg_hbm, su_hbm, wg_hbm, wu_hbm, wd_hbm,
    arr_hbm, dg_hbm, du_hbm, dd_hbm,
    bg, bt, cg, ct, part, og, tok, sg, su, wg, wu, wd, acc, fa, fb, gg, ug, ggt, ugt, hid,
    res, fin, pick_out, pick_in, ids_ref, slots_ref, gates_ref,
    rp1d, rp1b, rq1d, rq1b, rp2d, rp2b, rq2d, rq2b,
    ssem, rsem, lsem,
):
    f32 = jnp.float32
    bf = jnp.bfloat16
    width = bg.shape[-1]
    half_w = width // 2
    piece = half_w // PIECES
    hidden_n = sg.shape[0]
    pad = wg.shape[0] - hidden_n
    pcols, qcols = pl.ds(0, half_w), pl.ds(half_w, half_w)

    sections = lax.axis_size("section")
    sec = lax.axis_index("section")
    e = lax.axis_index("expert")
    y, x, z = e // 8, (e // 2) % 4, e % 2
    a = y // 2
    b = 1 - a
    p = (y + a) % 2
    q = 1 - p
    w = 1 - z
    xp, xm, xo = (x + 1) % 4, (x + 3) % 4, (x + 2) % 4
    before, after = (sec + sections - 1) % sections, (sec + 1) % sections

    def dev(y_, x_, z_):
        return (y_ * 4 + x_) * 2 + z_

    cross = dev(3 - y, x, z)
    y_dev = (sec, dev(2 * a + 1 - y % 2, x, z))
    z_dev = (sec, dev(y, x, w))
    xp_dev = (sec, dev(y, xp, z))
    xm_dev = (sec, dev(y, xm, z))
    c_dev = (sec, cross)

    local = []

    def fetch(src, dst):
        c = pltpu.make_async_copy(src, dst, lsem.at[len(local)])
        c.start()
        local.append(c)
        return c

    small_in = (fetch(ids_hbm, ids_ref), fetch(slots_hbm, slots_ref), fetch(gates_hbm, gates_ref))
    og_in = fetch(og_hbm, og)
    tok_in = fetch(tok_hbm, tok)
    sg_in = fetch(sg_hbm, sg)
    su_in = fetch(su_hbm, su)

    barrier = pltpu.get_barrier_semaphore()
    for d in (y_dev, z_dev, xp_dev, xm_dev, c_dev, (after, e), (after, cross)):
        pl.semaphore_signal(barrier, 1, device_id=d, device_id_type=pl.DeviceIdType.MESH)

    remote = []

    def send(src, dst, to):
        i = len(remote)
        c = pltpu.make_async_remote_copy(
            src_ref=src, dst_ref=dst, send_sem=ssem.at[i], recv_sem=rsem.at[i],
            device_id=to, device_id_type=pl.DeviceIdType.MESH,
        )
        c.start()
        remote.append(c)
        return c

    def arrived(copies):
        for c in copies:
            c.wait_recv()

    for c in small_in:
        c.wait()
    tokens_n = og.shape[0]
    rows32 = lax.broadcasted_iota(jnp.int32, (2 * CAP, tokens_n), 0)
    pick = jnp.zeros((2 * CAP, tokens_n), f32)
    scaled = jnp.zeros((2 * CAP, tokens_n), f32)
    for k in range(2):
        chosen = ids_ref[k:k + 1, :]
        base = jnp.where(chosen == a, 0, jnp.where(chosen == b, CAP, -CAP * CAP))
        hit = rows32 == base + slots_ref[k:k + 1, :]
        weight = gates_ref[k:k + 1, :].astype(f32) * (1.0 / 256.0)
        pick += jnp.where(hit, 1.0, 0.0)
        scaled += jnp.where(hit, weight, 0.0)
    pick = pick.astype(bf)
    scaled = scaled.astype(bf)
    pick_out[...] = pick

    def place(sel, src, buf, other):
        step = 1024
        for c in range(0, width, step):
            rows = jnp.dot(sel, src[:, c:c + step], preferred_element_type=f32)
            rows = rows.astype(bf)
            buf[p, a, x, z, :, c:c + step] = rows[:CAP]
            other[:, c:c + step] = rows[CAP:]

    og_in.wait()
    place(scaled, og, bg, cg)
    pl.semaphore_wait(barrier, 7)

    class Gather:
        def __init__(self, buf, other):
            self.buf, self.other = buf, other

        def own(self):
            buf = self.buf
            self.cross = send(self.other, buf.at[p, a, x, z], c_dev)
            self.one_a = self.one(a)

        def one(self, m):
            sp = self.buf.at[p, m, x, z, :, pcols]
            sq = self.buf.at[p, m, x, z, :, qcols]
            return (
                send(sp, sp, y_dev), send(sp, sp, z_dev),
                send(sq, sq, xp_dev), send(sq, sq, xm_dev),
            )

        def crossed(self):
            self.cross.wait_recv()
            self.one_b = self.one(b)

        def fwd1_a(self):
            arrived(self.one_a)
            s1 = self.buf.at[q, a, x, z, :, pcols]
            s2 = self.buf.at[p, a, xm, z, :, qcols]
            self.f1a = (send(s1, s1, z_dev), send(s2, s2, xp_dev))

        def fwd1_b(self):
            arrived(self.one_b)
            s1 = self.buf.at[p, b, x, w, :, pcols]
            s2 = self.buf.at[p, b, xp, z, :, qcols]
            self.f1b = (send(s1, s1, y_dev), send(s2, s2, xm_dev))

        def two(self, m):
            sp = self.buf.at[:, m, x, :, :, pcols]
            sq = self.buf.at[p, m, :, z, :, qcols]
            return (
                send(sp, sp, xp_dev), send(sp, sp, xm_dev),
                send(sq, sq, y_dev), send(sq, sq, z_dev),
            )

        def two_a(self):
            arrived(self.f1a)
            self.t_a = self.two(a)

        def two_b(self):
            arrived(self.f1b)
            self.t_b = self.two(b)

        def fwd2_a(self):
            arrived(self.t_a)
            s1 = self.buf.at[:, a, xm, :, :, pcols]
            s2 = self.buf.at[q, a, :, z, :, qcols]
            self.f2a = (send(s1, s1, xp_dev), send(s2, s2, z_dev))

        def fwd2_b(self):
            arrived(self.t_b)
            s1 = self.buf.at[:, b, xp, :, :, pcols]
            s2 = self.buf.at[p, b, :, w, :, qcols]
            self.f2b = (send(s1, s1, xm_dev), send(s2, s2, y_dev))

        def done(self):
            arrived(self.f2a + self.f2b)

    g = Gather(bg, cg)
    t = Gather(bt, ct)
    g.own()
    wd_in = fetch(wd_hbm, wd.at[pl.ds(0, hidden_n)])
    wg_in = fetch(wg_hbm, wg.at[pl.ds(0, hidden_n)])
    wu_in = fetch(wu_hbm, wu.at[pl.ds(0, hidden_n)])
    tok_in.wait()
    place(pick, tok, bt, ct)
    t.own()
    g.fwd1_a()
    g.crossed()
    t.fwd1_a()
    g.fwd1_b()
    g.two_a()
    t.crossed()
    g.two_b()
    t.fwd1_b()

    pick_sent = send(pick_out, pick_in, (before, e))

    sg_in.wait()
    su_in.wait()
    zeros = jnp.zeros((pad, 128), f32)
    for chunk in range(4):
        src = slice(128 * Y_OF_CHUNK[chunk], 128 * Y_OF_CHUNK[chunk] + 128)
        dst = slice(128 * chunk, 128 * chunk + 128)
        gate = sg[:, src].astype(f32)
        up = su[:, src].astype(f32)
        sig = 1.0 / (1.0 + jnp.exp(-gate))
        active = gate * sig
        hid[:, dst] = (active * up).astype(bf)
        slope = up * sig * (1.0 + gate * (1.0 - sig))
        fa[dst, :] = jnp.concatenate([slope, zeros], axis=0).T
        fb[dst, :] = jnp.concatenate([active, zeros], axis=0).T
    acc[...] = jnp.zeros_like(acc)
    for buf in (wd, wg, wu):
        buf[hidden_n:, :] = jnp.zeros((pad, width), bf)

    g.fwd2_a()
    t.two_a()
    wd_in.wait()
    g.fwd2_b()
    t.two_b()
    g.done()

    k_step = width // 4

    def hid_step(k, _):
        ks = pl.ds(pl.multiple_of(k * k_step, 128), k_step)
        rows = bg[:, :, :, :, :, ks].reshape(ROWS, k_step)
        acc[...] += lax.dot_general(
            rows, wd[:, ks], (((1,), (1,)), ((), ())), preferred_element_type=f32
        )
        return 0

    lax.fori_loop(0, 4, hid_step, 0)
    gg[...] = (acc[...] * fa[...]).astype(bf)
    ug[...] = (acc[...] * fb[...]).astype(bf)

    n_step = 512

    def parts(first):

        def part_step(n, _):
            ns = pl.ds(pl.multiple_of(first + n * n_step, 128), n_step)
            o = jnp.dot(gg[...], wg[:, ns], preferred_element_type=f32)
            o += jnp.dot(ug[...], wu[:, ns], preferred_element_type=f32)
            part[:, :, :, :, :, ns] = o.astype(bf).reshape(2, 2, 4, 2, CAP, n_step)
            return 0

        lax.fori_loop(0, piece // n_step, part_step, 0)

    def plus(dst, index, *others):
        total = dst[index].astype(f32)
        for o in others:
            total += o.astype(f32)
        dst[index] = total.astype(bf)

    def to_before(c):
        self_cols = c
        return (
            send(res.at[0, :, self_cols], fin.at[0, :, self_cols], (before, e)),
            send(res.at[1, :, self_cols], fin.at[1, :, self_cols], (before, cross)),
        )

    class ScatterP:
        def __init__(self, k):
            self.k, self.first = k, k * piece
            self.c = pl.ds(self.first, piece)

        def start(self):
            k, c = self.k, self.c
            parts(self.first)
            self.d1 = (
                send(part.at[:, a, xo, :, :, c], rp1d.at[k, 0], xp_dev),
                send(part.at[:, b, xo, :, :, c], rp1d.at[k, 1], xm_dev),
            )
            self.b1 = (
                send(part.at[:, b, xp, :, :, c], rp1b.at[k, 0, 1], xp_dev),
                send(part.at[:, a, xm, :, :, c], rp1b.at[k, 1, 0], xm_dev),
            )

        def diag1(self):
            k, c = self.k, self.c
            arrived(self.d1[:1])
            for i in range(2):
                for j in range(2):
                    plus(part, (i, a, xp, j, slice(None), c), rp1d[k, 0, i, j])
            s0 = send(part.at[:, a, xp, :, :, c], rp1b.at[k, 0, 0], xp_dev)
            arrived(self.d1[1:])
            for i in range(2):
                for j in range(2):
                    plus(part, (i, b, xm, j, slice(None), c), rp1d[k, 1, i, j])
            s1 = send(part.at[:, b, xm, :, :, c], rp1b.at[k, 1, 1], xm_dev)
            self.b1 += (s0, s1)

        def sum1(self):
            k, c = self.k, self.c
            arrived(self.b1)
            for i in range(2):
                for s, m in ((0, a), (1, b)):
                    for j in range(2):
                        plus(part, (i, m, x, j, slice(None), c), rp1b[k, 0, s, i, j], rp1b[k, 1, s, i, j])
            self.d2 = (
                send(part.at[q, a, x, w, :, c], rp2d.at[k, 0], y_dev),
                send(part.at[q, b, x, w, :, c], rp2d.at[k, 1], z_dev),
            )
            self.b2 = (
                send(part.at[p, b, x, w, :, c], rp2b.at[k, 0, 1], z_dev),
                send(part.at[q, a, x, z, :, c], rp2b.at[k, 1, 0], y_dev),
            )

        def diag2(self):
            k, c = self.k, self.c
            arrived(self.d2[:1])
            plus(part, (p, a, x, w, slice(None), c), rp2d[k, 0])
            s0 = send(part.at[p, a, x, w, :, c], rp2b.at[k, 0, 0], z_dev)
            arrived(self.d2[1:])
            plus(part, (q, b, x, z, slice(None), c), rp2d[k, 1])
            s1 = send(part.at[q, b, x, z, :, c], rp2b.at[k, 1, 1], y_dev)
            self.b2 += (s0, s1)

        def last(self):
            k, c = self.k, self.c
            arrived(self.b2)
            for s, m in ((0, a), (1, b)):
                res[s, :, c] = (
                    part[p, m, x, z, :, c].astype(f32)
                    + rp2b[k, 0, s].astype(f32) + rp2b[k, 1, s].astype(f32)
                ).astype(bf)
            self.out = to_before(c)

    class ScatterQ:
        def __init__(self, k):
            self.k, self.first = k, half_w + k * piece
            self.c = pl.ds(self.first, piece)

        def start(self):
            k, c = self.k, self.c
            parts(self.first)
            self.d1 = (
                send(part.at[q, a, :, w, :, c], rq1d.at[k, 0], y_dev),
                send(part.at[q, b, :, w, :, c], rq1d.at[k, 1], z_dev),
            )
            self.b1 = (
                send(part.at[p, b, :, w, :, c], rq1b.at[k, 0, 1], z_dev),
                send(part.at[q, a, :, z, :, c], rq1b.at[k, 1, 0], y_dev),
            )

        def diag1(self):
            k, c = self.k, self.c
            arrived(self.d1[:1])
            for i in range(4):
                plus(part, (p, a, i, w, slice(None), c), rq1d[k, 0, i])
            s0 = send(part.at[p, a, :, w, :, c], rq1b.at[k, 0, 0], z_dev)
            arrived(self.d1[1:])
            for i in range(4):
                plus(part, (q, b, i, z, slice(None), c), rq1d[k, 1, i])
            s1 = send(part.at[q, b, :, z, :, c], rq1b.at[k, 1, 1], y_dev)
            self.b1 += (s0, s1)

        def sum1(self):
            k, c = self.k, self.c
            arrived(self.b1)
            for i in range(4):
                for s, m in ((0, a), (1, b)):
                    plus(part, (p, m, i, z, slice(None), c), rq1b[k, 0, s, i], rq1b[k, 1, s, i])
            self.d2 = (
                send(part.at[p, a, xo, z, :, c], rq2d.at[k, 0], xp_dev),
                send(part.at[p, b, xo, z, :, c], rq2d.at[k, 1], xm_dev),
            )
            self.b2 = (
                send(part.at[p, b, xp, z, :, c], rq2b.at[k, 0, 1], xp_dev),
                send(part.at[p, a, xm, z, :, c], rq2b.at[k, 1, 0], xm_dev),
            )

        def diag2(self):
            k, c = self.k, self.c
            arrived(self.d2[:1])
            plus(part, (p, a, xp, z, slice(None), c), rq2d[k, 0])
            s0 = send(part.at[p, a, xp, z, :, c], rq2b.at[k, 0, 0], xp_dev)
            arrived(self.d2[1:])
            plus(part, (p, b, xm, z, slice(None), c), rq2d[k, 1])
            s1 = send(part.at[p, b, xm, z, :, c], rq2b.at[k, 1, 1], xm_dev)
            self.b2 += (s0, s1)

        def last(self):
            k, c = self.k, self.c
            arrived(self.b2)
            for s, m in ((0, a), (1, b)):
                res[s, :, c] = (
                    part[p, m, x, z, :, c].astype(f32)
                    + rq2b[k, 0, s].astype(f32) + rq2b[k, 1, s].astype(f32)
                ).astype(bf)
            self.out = to_before(c)

    def weight_grad(left, rows, out):

        def grad_step(n, _):
            ns = pl.ds(pl.multiple_of(n * n_step, 128), n_step)
            right = rows[:, :, :, :, :, ns].reshape(ROWS, n_step)
            out[pl.ds(0, hidden_n), ns] = jnp.dot(left[...], right, preferred_element_type=f32).astype(bf)
            return 0

        lax.fori_loop(0, width // n_step, grad_step, 0)

    ps = [ScatterP(k) for k in range(PIECES)]
    qs = [ScatterQ(k) for k in range(PIECES)]
    wg_in.wait()
    wu_in.wait()
    t.fwd2_a()
    ps[0].start()
    qs[0].start()
    ps[1].start()
    qs[1].start()
    ps[0].diag1()
    qs[0].diag1()
    ps[1].diag1()
    qs[1].diag1()
    t.fwd2_b()
    weight_grad(hid, bg, wd)
    dd_out = fetch(wd.at[pl.ds(0, hidden_n)], dd_hbm)
    ps[0].sum1()
    qs[0].sum1()
    ps[1].sum1()
    qs[1].sum1()
    for chunk in range(4):
        dst = slice(128 * chunk, 128 * chunk + 128)
        ggt[:, dst] = gg[dst, :].astype(f32).T[:hidden_n].astype(bf)
        ugt[:, dst] = ug[dst, :].astype(f32).T[:hidden_n].astype(bf)
    ps[0].diag2()
    qs[0].diag2()
    ps[1].diag2()
    qs[1].diag2()
    ps[0].last()
    qs[0].last()
    ps[1].last()
    qs[1].last()
    t.done()
    weight_grad(ggt, bt, wg)
    dg_out = fetch(wg.at[pl.ds(0, hidden_n)], dg_hbm)
    weight_grad(ugt, bt, wu)
    du_out = fetch(wu.at[pl.ds(0, hidden_n)], du_hbm)

    pick_sent.wait_recv()
    for scatter in ps + qs:
        arrived(scatter.out)
    took = jnp.where(sec == sections - 1, 0.0, pick_in[...].astype(f32)).T.astype(bf)
    step = 1024
    for c in range(0, width, step):
        rows = fin[:, :, c:c + step].reshape(2 * CAP, step)
        tok[:, c:c + step] = jnp.dot(took, rows, preferred_element_type=f32).astype(bf)
    arr_out = fetch(tok, arr_hbm)

    for c in remote:
        c.wait_send()
    for c in (dd_out, dg_out, du_out, arr_out):
        c.wait()


def exchange(ids, slots, gates, tok, og, sg, su, wg, wu, wd):
    width = tok.shape[-1]
    tokens_n = tok.shape[0]
    hidden_n = sg.shape[0]
    piece = width // 2 // PIECES
    f32, bf = jnp.float32, jnp.bfloat16
    rows_shape = (2, 2, 4, 2, CAP, width)
    padded = -(-hidden_n // 128) * 128
    any_spec = pl.BlockSpec(memory_space=pl.ANY)
    vm = pltpu.VMEM
    grad = jax.ShapeDtypeStruct((hidden_n, width), bf)
    return pl.pallas_call(
        kernel,
        name="exchange",
        out_shape=(jax.ShapeDtypeStruct((tokens_n, width), bf), grad, grad, grad),
        in_specs=[pl.BlockSpec(memory_space=pltpu.HBM)] * 10,
        out_specs=[any_spec] * 4,
        scratch_shapes=[
            vm(rows_shape, bf), vm(rows_shape, bf),
            vm((CAP, width), bf), vm((CAP, width), bf),
            vm(rows_shape, bf),
            vm((tokens_n, width), bf), vm((tokens_n, width), bf),
            vm((hidden_n, ROWS), bf), vm((hidden_n, ROWS), bf),
            vm((padded, width), bf), vm((padded, width), bf), vm((padded, width), bf),
            vm((ROWS, padded), f32), vm((ROWS, padded), f32), vm((ROWS, padded), f32),
            vm((ROWS, padded), bf), vm((ROWS, padded), bf),
            vm((hidden_n, ROWS), bf), vm((hidden_n, ROWS), bf), vm((hidden_n, ROWS), bf),
            vm((2, CAP, width), bf), vm((2, CAP, width), bf),
            vm((2 * CAP, tokens_n), bf), vm((2 * CAP, tokens_n), bf),
            vm(ids.shape, jnp.int32), vm(ids.shape, jnp.int32), vm(ids.shape, jnp.int32),
            vm((PIECES, 2, 2, 2, CAP, piece), bf), vm((PIECES, 2, 2, 2, 2, CAP, piece), bf),
            vm((PIECES, 2, 4, CAP, piece), bf), vm((PIECES, 2, 2, 4, CAP, piece), bf),
            vm((PIECES, 2, CAP, piece), bf), vm((PIECES, 2, 2, CAP, piece), bf),
            vm((PIECES, 2, CAP, piece), bf), vm((PIECES, 2, 2, CAP, piece), bf),
            pltpu.SemaphoreType.DMA((COPIES,)), pltpu.SemaphoreType.DMA((COPIES,)),
            pltpu.SemaphoreType.DMA((16,)),
        ],
        compiler_params=pltpu.CompilerParams(
            collective_id=0, has_side_effects=True, vmem_limit_bytes=VMEM_MIB << 20
        ),
        cost_estimate=pl.CostEstimate(
            flops=12 * ROWS * hidden_n * width, transcendentals=ROWS * hidden_n,
            bytes_accessed=24 << 20,
        ),
    )(ids, slots, gates, tok, og, sg, su, wg, wu, wd)


def store_kernel(*refs):
    ins, outs, sem = refs[:4], refs[4:8], refs[8]
    copies = []
    for src, dst in zip(ins, outs):
        rows = src.shape[0]
        for first in range(0, rows, rows // 2):
            part = pl.ds(first, rows // 2)
            copies.append(pltpu.make_async_copy(src.at[part], dst.at[part], sem.at[len(copies)]))
            copies[-1].start()
    for c in copies:
        c.wait()


def store(*arrays):
    size = sum(v.size for v in arrays)
    return pl.pallas_call(
        store_kernel,
        name="store",
        out_shape=tuple(jax.ShapeDtypeStruct(v.shape, v.dtype) for v in arrays),
        in_specs=[pl.BlockSpec(memory_space=pl.ANY)] * 4,
        out_specs=[pl.BlockSpec(memory_space=pltpu.HBM)] * 4,
        scratch_shapes=[pltpu.SemaphoreType.DMA((8,))],
        compiler_params=pltpu.CompilerParams(vmem_limit_bytes=1 << 20),
        cost_estimate=pl.CostEstimate(flops=0, transcendentals=0, bytes_accessed=4 * size),
    )(*arrays)


def shards(
    tokens, out_grad, expert_ids, slot_ids, gate_int, saved_gate, saved_up, w_gate, w_up, w_down
):
    arriving, grad_gate, grad_up, grad_down = exchange(
        *[pltpu.with_memory_space_constraint(v, pltpu.HBM) for v in (expert_ids[0].T, slot_ids[0].T, gate_int[0].T, tokens[0], out_grad[0],
        saved_gate[0].T, saved_up[0].T, w_gate[0].T, w_up[0].T, w_down[0])],
    )
    arriving, grad_gate, grad_up, grad_down = store(arriving, grad_gate, grad_up, grad_down)
    return (arriving[None], grad_gate.T[None], grad_up.T[None], grad_down[None])


def solution(mesh):
    row = P("section", "expert", None)
    col = P("section", None, "expert")
    return jax.shard_map(
        shards,
        mesh=mesh,
        in_specs=(row,) * 5 + (col,) * 4 + (row,),
        out_specs=(row, col, col, row),
        check_vma=False,
    )
```

```python
import jax
import jax.numpy as jnp
from jax import lax
from jax.experimental import pallas as pl
from jax.experimental.pallas import tpu as pltpu
from jax.sharding import PartitionSpec as P

CAP = 16
ROWS = 512
Y_OF_CHUNK = (0, 3, 1, 2)
COPIES = 112
PIECES = 2
VMEM_MIB = 40


def kernel(
    ids_hbm, slots_hbm, gates_hbm, tok_hbm, og_hbm, sg_hbm, su_hbm, wg_hbm, wu_hbm, wd_hbm,
    arr_hbm, dg_hbm, du_hbm, dd_hbm,
    bg, bt, cg, ct, part, og, tok, sg, su, wg, wu, wd, acc, fa, fb, gg, ug, ggt, ugt, hid,
    res, fin, pick_out, pick_in, ids_ref, slots_ref, gates_ref,
    rp1d, rp1b, rq1d, rq1b, rp2d, rp2b, rq2d, rq2b,
    ssem, rsem, lsem,
):
    f32 = jnp.float32
    bf = jnp.bfloat16
    width = bg.shape[-1]
    half_w = width // 2
    piece = half_w // PIECES
    hidden_n = sg.shape[0]
    pad = wg.shape[0] - hidden_n
    pcols, qcols = pl.ds(0, half_w), pl.ds(half_w, half_w)

    sections = lax.axis_size("section")
    sec = lax.axis_index("section")
    e = lax.axis_index("expert")
    y, x, z = e // 8, (e // 2) % 4, e % 2
    a = y // 2
    b = 1 - a
    p = (y + a) % 2
    q = 1 - p
    w = 1 - z
    xp, xm, xo = (x + 1) % 4, (x + 3) % 4, (x + 2) % 4
    before, after = (sec + sections - 1) % sections, (sec + 1) % sections

    def dev(y_, x_, z_):
        return (y_ * 4 + x_) * 2 + z_

    cross = dev(3 - y, x, z)
    y_dev = (sec, dev(2 * a + 1 - y % 2, x, z))
    z_dev = (sec, dev(y, x, w))
    xp_dev = (sec, dev(y, xp, z))
    xm_dev = (sec, dev(y, xm, z))
    c_dev = (sec, cross)

    local = []

    def fetch(src, dst):
        c = pltpu.make_async_copy(src, dst, lsem.at[len(local)])
        c.start()
        local.append(c)
        return c

    small_in = (fetch(ids_hbm, ids_ref), fetch(slots_hbm, slots_ref), fetch(gates_hbm, gates_ref))
    og_in = fetch(og_hbm, og)
    tok_in = fetch(tok_hbm, tok)
    sg_in = fetch(sg_hbm, sg)
    su_in = fetch(su_hbm, su)

    barrier = pltpu.get_barrier_semaphore()
    for d in (y_dev, z_dev, xp_dev, xm_dev, c_dev, (after, e), (after, cross)):
        pl.semaphore_signal(barrier, 1, device_id=d, device_id_type=pl.DeviceIdType.MESH)

    remote = []

    def send(src, dst, to):
        i = len(remote)
        c = pltpu.make_async_remote_copy(
            src_ref=src, dst_ref=dst, send_sem=ssem.at[i], recv_sem=rsem.at[i],
            device_id=to, device_id_type=pl.DeviceIdType.MESH,
        )
        c.start()
        remote.append(c)
        return c

    def arrived(copies):
        for c in copies:
            c.wait_recv()

    for c in small_in:
        c.wait()
    tokens_n = og.shape[0]
    rows32 = lax.broadcasted_iota(jnp.int32, (2 * CAP, tokens_n), 0)
    pick = jnp.zeros((2 * CAP, tokens_n), f32)
    scaled = jnp.zeros((2 * CAP, tokens_n), f32)
    for k in range(2):
        chosen = ids_ref[k:k + 1, :]
        base = jnp.where(chosen == a, 0, jnp.where(chosen == b, CAP, -CAP * CAP))
        hit = rows32 == base + slots_ref[k:k + 1, :]
        weight = gates_ref[k:k + 1, :].astype(f32) * (1.0 / 256.0)
        pick += jnp.where(hit, 1.0, 0.0)
        scaled += jnp.where(hit, weight, 0.0)
    pick = pick.astype(bf)
    scaled = scaled.astype(bf)
    pick_out[...] = pick

    def place(sel, src, buf, other):
        step = 1024
        for c in range(0, width, step):
            rows = jnp.dot(sel, src[:, c:c + step], preferred_element_type=f32)
            rows = rows.astype(bf)
            buf[p, a, x, z, :, c:c + step] = rows[:CAP]
            other[:, c:c + step] = rows[CAP:]

    og_in.wait()
    place(scaled, og, bg, cg)
    pl.semaphore_wait(barrier, 7)

    class Gather:
        def __init__(self, buf, other):
            self.buf, self.other = buf, other

        def own(self):
            buf = self.buf
            self.cross = send(self.other, buf.at[p, a, x, z], c_dev)
            self.one_a = self.one(a)

        def one(self, m):
            sp = self.buf.at[p, m, x, z, :, pcols]
            sq = self.buf.at[p, m, x, z, :, qcols]
            return (
                send(sp, sp, y_dev), send(sp, sp, z_dev),
                send(sq, sq, xp_dev), send(sq, sq, xm_dev),
            )

        def crossed(self):
            self.cross.wait_recv()
            self.one_b = self.one(b)

        def fwd1_a(self):
            arrived(self.one_a)
            s1 = self.buf.at[q, a, x, z, :, pcols]
            s2 = self.buf.at[p, a, xm, z, :, qcols]
            self.f1a = (send(s1, s1, z_dev), send(s2, s2, xp_dev))

        def fwd1_b(self):
            arrived(self.one_b)
            s1 = self.buf.at[p, b, x, w, :, pcols]
            s2 = self.buf.at[p, b, xp, z, :, qcols]
            self.f1b = (send(s1, s1, y_dev), send(s2, s2, xm_dev))

        def two(self, m):
            sp = self.buf.at[:, m, x, :, :, pcols]
            sq = self.buf.at[p, m, :, z, :, qcols]
            return (
                send(sp, sp, xp_dev), send(sp, sp, xm_dev),
                send(sq, sq, y_dev), send(sq, sq, z_dev),
            )

        def two_a(self):
            arrived(self.f1a)
            self.t_a = self.two(a)

        def two_b(self):
            arrived(self.f1b)
            self.t_b = self.two(b)

        def fwd2_a(self):
            arrived(self.t_a)
            s1 = self.buf.at[:, a, xm, :, :, pcols]
            s2 = self.buf.at[q, a, :, z, :, qcols]
            self.f2a = (send(s1, s1, xp_dev), send(s2, s2, z_dev))

        def fwd2_b(self):
            arrived(self.t_b)
            s1 = self.buf.at[:, b, xp, :, :, pcols]
            s2 = self.buf.at[p, b, :, w, :, qcols]
            self.f2b = (send(s1, s1, xm_dev), send(s2, s2, y_dev))

        def done(self):
            arrived(self.f2a + self.f2b)

    g = Gather(bg, cg)
    t = Gather(bt, ct)
    g.own()
    wd_in = fetch(wd_hbm, wd.at[pl.ds(0, hidden_n)])
    wg_in = fetch(wg_hbm, wg.at[pl.ds(0, hidden_n)])
    wu_in = fetch(wu_hbm, wu.at[pl.ds(0, hidden_n)])
    tok_in.wait()
    place(pick, tok, bt, ct)
    t.own()
    g.fwd1_a()
    g.crossed()
    t.fwd1_a()
    g.fwd1_b()
    g.two_a()
    t.crossed()
    g.two_b()
    t.fwd1_b()

    pick_sent = send(pick_out, pick_in, (before, e))

    sg_in.wait()
    su_in.wait()
    zeros = jnp.zeros((pad, 128), f32)
    for chunk in range(4):
        src = slice(128 * Y_OF_CHUNK[chunk], 128 * Y_OF_CHUNK[chunk] + 128)
        dst = slice(128 * chunk, 128 * chunk + 128)
        gate = sg[:, src].astype(f32)
        up = su[:, src].astype(f32)
        sig = 1.0 / (1.0 + jnp.exp(-gate))
        active = gate * sig
        hid[:, dst] = (active * up).astype(bf)
        slope = up * sig * (1.0 + gate * (1.0 - sig))
        fa[dst, :] = jnp.concatenate([slope, zeros], axis=0).T
        fb[dst, :] = jnp.concatenate([active, zeros], axis=0).T
    acc[...] = jnp.zeros_like(acc)
    for buf in (wd, wg, wu):
        buf[hidden_n:, :] = jnp.zeros((pad, width), bf)

    g.fwd2_a()
    wd_in.wait()
    g.fwd2_b()
    t.two_a()
    t.two_b()
    g.done()

    k_step = width // 4

    def hid_step(k, _):
        ks = pl.ds(pl.multiple_of(k * k_step, 128), k_step)
        rows = bg[:, :, :, :, :, ks].reshape(ROWS, k_step)
        acc[...] += lax.dot_general(
            rows, wd[:, ks], (((1,), (1,)), ((), ())), preferred_element_type=f32
        )
        return 0

    lax.fori_loop(0, 4, hid_step, 0)
    gg[...] = (acc[...] * fa[...]).astype(bf)
    ug[...] = (acc[...] * fb[...]).astype(bf)

    n_step = 512

    def parts(first):

        def part_step(n, _):
            ns = pl.ds(pl.multiple_of(first + n * n_step, 128), n_step)
            o = jnp.dot(gg[...], wg[:, ns], preferred_element_type=f32)
            o += jnp.dot(ug[...], wu[:, ns], preferred_element_type=f32)
            part[:, :, :, :, :, ns] = o.astype(bf).reshape(2, 2, 4, 2, CAP, n_step)
            return 0

        lax.fori_loop(0, piece // n_step, part_step, 0)

    def plus(dst, index, *others):
        total = dst[index].astype(f32)
        for o in others:
            total += o.astype(f32)
        dst[index] = total.astype(bf)

    def to_before(c):
        self_cols = c
        return (
            send(res.at[0, :, self_cols], fin.at[0, :, self_cols], (before, e)),
            send(res.at[1, :, self_cols], fin.at[1, :, self_cols], (before, cross)),
        )

    class ScatterP:
        def __init__(self, k):
            self.k, self.first = k, k * piece
            self.c = pl.ds(self.first, piece)

        def start(self):
            k, c = self.k, self.c
            parts(self.first)
            self.d1 = (
                send(part.at[:, a, xo, :, :, c], rp1d.at[k, 0], xp_dev),
                send(part.at[:, b, xo, :, :, c], rp1d.at[k, 1], xm_dev),
            )
            self.b1 = (
                send(part.at[:, b, xp, :, :, c], rp1b.at[k, 0, 1], xp_dev),
                send(part.at[:, a, xm, :, :, c], rp1b.at[k, 1, 0], xm_dev),
            )

        def diag1(self):
            k, c = self.k, self.c
            arrived(self.d1[:1])
            for i in range(2):
                for j in range(2):
                    plus(part, (i, a, xp, j, slice(None), c), rp1d[k, 0, i, j])
            s0 = send(part.at[:, a, xp, :, :, c], rp1b.at[k, 0, 0], xp_dev)
            arrived(self.d1[1:])
            for i in range(2):
                for j in range(2):
                    plus(part, (i, b, xm, j, slice(None), c), rp1d[k, 1, i, j])
            s1 = send(part.at[:, b, xm, :, :, c], rp1b.at[k, 1, 1], xm_dev)
            self.b1 += (s0, s1)

        def sum1(self):
            k, c = self.k, self.c
            arrived(self.b1)
            for i in range(2):
                for s, m in ((0, a), (1, b)):
                    for j in range(2):
                        plus(part, (i, m, x, j, slice(None), c), rp1b[k, 0, s, i, j], rp1b[k, 1, s, i, j])
            self.d2 = (
                send(part.at[q, a, x, w, :, c], rp2d.at[k, 0], y_dev),
                send(part.at[q, b, x, w, :, c], rp2d.at[k, 1], z_dev),
            )
            self.b2 = (
                send(part.at[p, b, x, w, :, c], rp2b.at[k, 0, 1], z_dev),
                send(part.at[q, a, x, z, :, c], rp2b.at[k, 1, 0], y_dev),
            )

        def diag2(self):
            k, c = self.k, self.c
            arrived(self.d2[:1])
            plus(part, (p, a, x, w, slice(None), c), rp2d[k, 0])
            s0 = send(part.at[p, a, x, w, :, c], rp2b.at[k, 0, 0], z_dev)
            arrived(self.d2[1:])
            plus(part, (q, b, x, z, slice(None), c), rp2d[k, 1])
            s1 = send(part.at[q, b, x, z, :, c], rp2b.at[k, 1, 1], y_dev)
            self.b2 += (s0, s1)

        def last(self):
            k, c = self.k, self.c
            arrived(self.b2)
            for s, m in ((0, a), (1, b)):
                res[s, :, c] = (
                    part[p, m, x, z, :, c].astype(f32)
                    + rp2b[k, 0, s].astype(f32) + rp2b[k, 1, s].astype(f32)
                ).astype(bf)
            self.out = to_before(c)

    class ScatterQ:
        def __init__(self, k):
            self.k, self.first = k, half_w + k * piece
            self.c = pl.ds(self.first, piece)

        def start(self):
            k, c = self.k, self.c
            parts(self.first)
            self.d1 = (
                send(part.at[q, a, :, w, :, c], rq1d.at[k, 0], y_dev),
                send(part.at[q, b, :, w, :, c], rq1d.at[k, 1], z_dev),
            )
            self.b1 = (
                send(part.at[p, b, :, w, :, c], rq1b.at[k, 0, 1], z_dev),
                send(part.at[q, a, :, z, :, c], rq1b.at[k, 1, 0], y_dev),
            )

        def diag1(self):
            k, c = self.k, self.c
            arrived(self.d1[:1])
            for i in range(4):
                plus(part, (p, a, i, w, slice(None), c), rq1d[k, 0, i])
            s0 = send(part.at[p, a, :, w, :, c], rq1b.at[k, 0, 0], z_dev)
            arrived(self.d1[1:])
            for i in range(4):
                plus(part, (q, b, i, z, slice(None), c), rq1d[k, 1, i])
            s1 = send(part.at[q, b, :, z, :, c], rq1b.at[k, 1, 1], y_dev)
            self.b1 += (s0, s1)

        def sum1(self):
            k, c = self.k, self.c
            arrived(self.b1)
            for i in range(4):
                for s, m in ((0, a), (1, b)):
                    plus(part, (p, m, i, z, slice(None), c), rq1b[k, 0, s, i], rq1b[k, 1, s, i])
            self.d2 = (
                send(part.at[p, a, xo, z, :, c], rq2d.at[k, 0], xp_dev),
                send(part.at[p, b, xo, z, :, c], rq2d.at[k, 1], xm_dev),
            )
            self.b2 = (
                send(part.at[p, b, xp, z, :, c], rq2b.at[k, 0, 1], xp_dev),
                send(part.at[p, a, xm, z, :, c], rq2b.at[k, 1, 0], xm_dev),
            )

        def diag2(self):
            k, c = self.k, self.c
            arrived(self.d2[:1])
            plus(part, (p, a, xp, z, slice(None), c), rq2d[k, 0])
            s0 = send(part.at[p, a, xp, z, :, c], rq2b.at[k, 0, 0], xp_dev)
            arrived(self.d2[1:])
            plus(part, (p, b, xm, z, slice(None), c), rq2d[k, 1])
            s1 = send(part.at[p, b, xm, z, :, c], rq2b.at[k, 1, 1], xm_dev)
            self.b2 += (s0, s1)

        def last(self):
            k, c = self.k, self.c
            arrived(self.b2)
            for s, m in ((0, a), (1, b)):
                res[s, :, c] = (
                    part[p, m, x, z, :, c].astype(f32)
                    + rq2b[k, 0, s].astype(f32) + rq2b[k, 1, s].astype(f32)
                ).astype(bf)
            self.out = to_before(c)

    stored = []

    def weight_grad(left, rows, out, result, low, high):

        def grad_step(n, _):
            ns = pl.ds(pl.multiple_of(n * n_step, 128), n_step)
            right = rows[:, :, :, :, :, ns].reshape(ROWS, n_step)
            out[pl.ds(0, hidden_n), ns] = jnp.dot(left[...], right, preferred_element_type=f32).astype(bf)
            return 0

        lax.fori_loop(low * width // 4 // n_step, high * width // 4 // n_step, grad_step, 0)
        done = pl.ds(low * width // 4, (high - low) * width // 4)
        stored.append(fetch(out.at[pl.ds(0, hidden_n), done], result.at[:, done]))

    ps = [ScatterP(k) for k in range(PIECES)]
    qs = [ScatterQ(k) for k in range(PIECES)]
    wg_in.wait()
    wu_in.wait()
    t.fwd2_a()
    ps[0].start()
    qs[0].start()
    ps[1].start()
    qs[1].start()
    ps[0].diag1()
    qs[0].diag1()
    ps[1].diag1()
    qs[1].diag1()
    t.fwd2_b()
    weight_grad(hid, bg, wd, dd_hbm, 0, 4)
    ps[0].sum1()
    qs[0].sum1()
    ps[1].sum1()
    qs[1].sum1()
    for chunk in range(4):
        dst = slice(128 * chunk, 128 * chunk + 128)
        ggt[:, dst] = gg[dst, :].astype(f32).T[:hidden_n].astype(bf)
        ugt[:, dst] = ug[dst, :].astype(f32).T[:hidden_n].astype(bf)
    ps[0].diag2()
    qs[0].diag2()
    ps[1].diag2()
    qs[1].diag2()
    t.done()
    weight_grad(ggt, bt, wg, dg_hbm, 0, 2)
    ps[0].last()
    qs[0].last()
    ps[1].last()
    qs[1].last()
    weight_grad(ggt, bt, wg, dg_hbm, 2, 4)
    weight_grad(ugt, bt, wu, du_hbm, 0, 2)
    weight_grad(ugt, bt, wu, du_hbm, 2, 4)

    pick_sent.wait_recv()
    for scatter in ps + qs:
        arrived(scatter.out)
    took = jnp.where(sec == sections - 1, 0.0, pick_in[...].astype(f32)).T.astype(bf)
    step = 1024
    for c in range(0, width, step):
        rows = fin[:, :, c:c + step].reshape(2 * CAP, step)
        tok[:, c:c + step] = jnp.dot(took, rows, preferred_element_type=f32).astype(bf)
    arr_out = fetch(tok, arr_hbm)

    for c in remote:
        c.wait_send()
    for c in stored + [arr_out]:
        c.wait()


def exchange(ids, slots, gates, tok, og, sg, su, wg, wu, wd):
    width = tok.shape[-1]
    tokens_n = tok.shape[0]
    hidden_n = sg.shape[0]
    piece = width // 2 // PIECES
    f32, bf = jnp.float32, jnp.bfloat16
    rows_shape = (2, 2, 4, 2, CAP, width)
    padded = -(-hidden_n // 128) * 128
    any_spec = pl.BlockSpec(memory_space=pl.ANY)
    vm = pltpu.VMEM
    grad = jax.ShapeDtypeStruct((hidden_n, width), bf)
    return pl.pallas_call(
        kernel,
        name="exchange",
        out_shape=(jax.ShapeDtypeStruct((tokens_n, width), bf), grad, grad, grad),
        in_specs=[pl.BlockSpec(memory_space=pltpu.HBM)] * 10,
        out_specs=[any_spec] * 4,
        scratch_shapes=[
            vm(rows_shape, bf), vm(rows_shape, bf),
            vm((CAP, width), bf), vm((CAP, width), bf),
            vm(rows_shape, bf),
            vm((tokens_n, width), bf), vm((tokens_n, width), bf),
            vm((hidden_n, ROWS), bf), vm((hidden_n, ROWS), bf),
            vm((padded, width), bf), vm((padded, width), bf), vm((padded, width), bf),
            vm((ROWS, padded), f32), vm((ROWS, padded), f32), vm((ROWS, padded), f32),
            vm((ROWS, padded), bf), vm((ROWS, padded), bf),
            vm((hidden_n, ROWS), bf), vm((hidden_n, ROWS), bf), vm((hidden_n, ROWS), bf),
            vm((2, CAP, width), bf), vm((2, CAP, width), bf),
            vm((2 * CAP, tokens_n), bf), vm((2 * CAP, tokens_n), bf),
            vm(ids.shape, jnp.int32), vm(ids.shape, jnp.int32), vm(ids.shape, jnp.int32),
            vm((PIECES, 2, 2, 2, CAP, piece), bf), vm((PIECES, 2, 2, 2, 2, CAP, piece), bf),
            vm((PIECES, 2, 4, CAP, piece), bf), vm((PIECES, 2, 2, 4, CAP, piece), bf),
            vm((PIECES, 2, CAP, piece), bf), vm((PIECES, 2, 2, CAP, piece), bf),
            vm((PIECES, 2, CAP, piece), bf), vm((PIECES, 2, 2, CAP, piece), bf),
            pltpu.SemaphoreType.DMA((COPIES,)), pltpu.SemaphoreType.DMA((COPIES,)),
            pltpu.SemaphoreType.DMA((24,)),
        ],
        compiler_params=pltpu.CompilerParams(
            collective_id=0, has_side_effects=True, vmem_limit_bytes=VMEM_MIB << 20
        ),
        cost_estimate=pl.CostEstimate(
            flops=12 * ROWS * hidden_n * width, transcendentals=ROWS * hidden_n,
            bytes_accessed=24 << 20,
        ),
    )(ids, slots, gates, tok, og, sg, su, wg, wu, wd)


def store_kernel(*refs):
    ins, outs, sem = refs[:4], refs[4:8], refs[8]
    copies = []
    for src, dst in zip(ins, outs):
        rows = src.shape[0]
        for first in range(0, rows, rows // 2):
            part = pl.ds(first, rows // 2)
            copies.append(pltpu.make_async_copy(src.at[part], dst.at[part], sem.at[len(copies)]))
            copies[-1].start()
    for c in copies:
        c.wait()


def store(*arrays):
    size = sum(v.size for v in arrays)
    return pl.pallas_call(
        store_kernel,
        name="store",
        out_shape=tuple(jax.ShapeDtypeStruct(v.shape, v.dtype) for v in arrays),
        in_specs=[pl.BlockSpec(memory_space=pl.ANY)] * 4,
        out_specs=[pl.BlockSpec(memory_space=pltpu.HBM)] * 4,
        scratch_shapes=[pltpu.SemaphoreType.DMA((8,))],
        compiler_params=pltpu.CompilerParams(vmem_limit_bytes=1 << 20),
        cost_estimate=pl.CostEstimate(flops=0, transcendentals=0, bytes_accessed=4 * size),
    )(*arrays)


def shards(
    tokens, out_grad, expert_ids, slot_ids, gate_int, saved_gate, saved_up, w_gate, w_up, w_down
):
    arriving, grad_gate, grad_up, grad_down = exchange(
        *[pltpu.with_memory_space_constraint(v, pltpu.HBM) for v in (expert_ids[0].T, slot_ids[0].T, gate_int[0].T, tokens[0], out_grad[0],
        saved_gate[0].T, saved_up[0].T, w_gate[0].T, w_up[0].T, w_down[0])],
    )
    arriving, grad_gate, grad_up, grad_down = store(arriving, grad_gate, grad_up, grad_down)
    return (arriving[None], grad_gate.T[None], grad_up.T[None], grad_down[None])


def solution(mesh):
    row = P("section", "expert", None)
    col = P("section", None, "expert")
    return jax.shard_map(
        shards,
        mesh=mesh,
        in_specs=(row,) * 5 + (col,) * 4 + (row,),
        out_specs=(row, col, col, row),
        check_vma=False,
    )
```
